32 devices in a mesh: proto: 8 (over z, y), patch: 4 (over x, core).
Axes of the slice: x: 2, y: 2, z: 4, core: 2. Of those that a mesh axis runs over, the one named last changes fastest.
Arguments:
- teacher_feats: bfloat16 [8192, 256], P('patch'), may hold values from -6 to 6
- student_feats: bfloat16 [8192, 256], P('patch'), may hold values from -6 to 6
- masked: int32 [32, 128], P('patch'), may hold values from 0 to 255, as said below
- progress_counter: int32 [1], replicated, may hold values from 0 to 30
- prototypes: bfloat16 [256, 8192], P(None, 'proto'), may hold values from -1 to 1
Outputs:
- patch_loss: float32 [4096], P('patch')
- grad_student: float32 [4096, 256], P(('patch', 'proto'))
- grad_protos: float32 [256, 8192], P('patch', 'proto')
The draws below stay inside these ranges and needn't reach their ends.
Inputs may be any that keep to these rules, and one draw needn't show every extreme that they name: `masked`: each row holds 128 distinct patch indices of one image.
All inputs are finite; a program needn't handle non-finite values.
Results may differ from the reference program's by a relative error of at most 0.0069.
Values sent between devices are 32-bit elements; how exact they have to be, the bound alone decides.
A program may use at most 64 MiB of HBM per device.

```python
import jax
import jax.numpy as jnp
from jax import lax

K = 256
NPATCH = 256
C_DEV = 1024
ITERS = 3
HEATUP_LENGTH = 30
MASK = 128
IMG_DEV = 8
PROTOS = 8192
IMAGES = 32
MASKED = 4096


def shared_centres(key):
    centres = jax.random.normal(jax.random.fold_in(key, 101), (16, K), jnp.float32)
    return jnp.clip(centres, -3.0, 3.0)


def draw_masked(key, part):
    keys_list = jax.random.split(jax.random.fold_in(key, 7), IMAGES)

    def one_image(image_key):
        return jax.random.permutation(image_key, NPATCH)[:MASK]
    return jax.vmap(one_image)(keys_list).astype(jnp.int32)


def draw_teacher_feats(key, part):
    total_rows = IMAGES * NPATCH
    shard_total = IMAGES // IMG_DEV
    centres = shared_centres(key)
    subkeys = jax.random.split(jax.random.fold_in(key, 211), 6)
    favourite = jax.random.randint(subkeys[0], (shard_total,), 0, 16)
    shard_of_row = jnp.arange(total_rows) // (IMG_DEV * NPATCH)
    own_centre = favourite[shard_of_row]
    other_centre = jnp.minimum(jax.random.randint(subkeys[1], (total_rows,), 0, 16), jax.random.randint(subkeys[2], (total_rows,), 0, 16))
    lottery = jax.random.randint(subkeys[3], (total_rows,), 0, 10)
    chosen = jnp.where(lottery < 6, own_centre, other_centre)
    mixing = jax.random.uniform(subkeys[4], (total_rows, 1), jnp.float32, 0.35, 0.7)
    random_part = jax.random.normal(subkeys[5], (total_rows, K), jnp.float32)
    values = 3.0 * (mixing * centres[chosen] + jnp.sqrt(1.0 - mixing * mixing) * random_part)
    return jnp.clip(values, -6.0, 6.0).astype(jnp.bfloat16)


def draw_prototypes(key, part):
    shard_total = PROTOS // C_DEV
    centres = shared_centres(key)
    subkeys = jax.random.split(jax.random.fold_in(key, 307), 5)
    shard_centre = jax.random.randint(subkeys[0], (shard_total,), 0, 16)
    shard_of_column = jnp.arange(PROTOS) // C_DEV
    own_centre = shard_centre[shard_of_column]
    other_centre = jax.random.randint(subkeys[1], (PROTOS,), 0, 16)
    lottery = jax.random.randint(subkeys[2], (PROTOS,), 0, 4)
    chosen = jnp.where(lottery < 3, own_centre, other_centre)
    mixing = jax.random.uniform(subkeys[3], (PROTOS, 1), jnp.float32, 0.3, 0.6)
    random_part = jax.random.normal(subkeys[4], (PROTOS, K), jnp.float32)
    values = (mixing * centres[chosen] + jnp.sqrt(1.0 - mixing * mixing) * random_part) * K ** (-0.5)
    return jnp.clip(values, -1.0, 1.0).T.astype(jnp.bfloat16)


def steps_of(key, dims, cuts, low, high):
    level = 1.0
    for dim, shards_of in cuts:
        steps = jax.random.uniform(jax.random.fold_in(jax.random.fold_in(key, 6), dim), (shards_of,), jnp.float32, low / len(cuts), high / len(cuts))
        level = level * jnp.repeat(jnp.exp(steps), dims[dim] // shards_of).reshape((-1,) + (1,) * (len(dims) - 1 - dim))
    return level


def scatter_about(rng, extent, spread, bound, cuts=(), kind=jnp.bfloat16):
    gain = steps_of(rng, extent, cuts, -0.22, 0.18) if cuts else 1.0
    values = jax.random.normal(rng, extent, jnp.float32) * spread * gain
    return jnp.minimum(jnp.maximum(values, -bound), bound).astype(kind)


def setup_inputs(seed: int = 0) -> dict:
    seeds = jax.random.split(jax.random.key(seed), 6)
    teacher_feats = draw_teacher_feats(jax.random.fold_in(seeds[5], 71), 0)
    student_feats = scatter_about(seeds[1], (IMAGES * NPATCH, K), 1.0, 6.0, ((0, 4),))
    masked = draw_masked(jax.random.fold_in(seeds[5], 71), 0)
    progress_counter = jax.random.randint(seeds[3], (1,), 0, HEATUP_LENGTH + 1).astype(jnp.int32)
    prototypes = draw_prototypes(jax.random.fold_in(seeds[5], 71), 0)
    return {"teacher_feats": teacher_feats, "student_feats": student_feats, "masked": masked, "progress_counter": progress_counter, "prototypes": prototypes}


def unit_rows(x):
    return x * lax.rsqrt(lax.optimization_barrier(jnp.sum(x * x, axis=-1, keepdims=True)) + 1e-12)

def unit_cols(w):
    return w * lax.rsqrt(lax.optimization_barrier(jnp.sum(w * w, axis=0, keepdims=True)) + 1e-12)

def reference(teacher_feats, student_feats, masked, progress_counter, prototypes):
    image_base = (jnp.arange(IMAGES).astype(jnp.int32) * NPATCH)[:, None]
    slot_rows = (image_base + masked.astype(jnp.int32)).reshape(-1)
    teacher_rows = teacher_feats[slot_rows].astype(jnp.float32)
    student_rows = student_feats[slot_rows].astype(jnp.float32)
    mentor_unitlength = unit_rows(teacher_rows).astype(jnp.bfloat16)
    s_full, pull_s = jax.vjp(unit_rows, student_rows)
    s_hat = s_full.astype(jnp.bfloat16)
    w_full, pull_w = jax.vjp(unit_cols, prototypes.astype(jnp.float32))
    prototype_normalized = w_full.astype(jnp.bfloat16)
    sharpness_divisor = 0.04 + 0.03 * progress_counter[0].astype(jnp.float32) / HEATUP_LENGTH
    blocks = PROTOS // C_DEV
    block_ids = jnp.arange(blocks).astype(jnp.int32)

    def teacher_block(block_index):
        centroid_tile = lax.dynamic_slice_in_dim(prototype_normalized, block_index * C_DEV, C_DEV, 1)
        return jnp.exp(jnp.dot(mentor_unitlength, centroid_tile, preferred_element_type=jnp.float32) / sharpness_divisor)

    def balancing_sweep(column_factor):

        def sweep_step(carried, block_index):
            eblock = teacher_block(block_index)
            ablock = 1.0 / jnp.dot(column_factor, eblock, precision=lax.Precision.HIGHEST)
            return (carried + jnp.dot(eblock, ablock, precision=lax.Precision.HIGHEST), ablock)
        col_denom, ablocks = lax.scan(sweep_step, jnp.zeros((MASKED,), jnp.float32), block_ids)
        return (ablocks.reshape(-1), 1.0 / col_denom)
    column_factor = jnp.ones((MASKED,), jnp.float32)
    row_factor = jnp.ones((PROTOS,), jnp.float32)
    for iteration in range(ITERS):
        row_factor, column_factor = balancing_sweep(column_factor)

    def total_step(carried, block_index):
        centroid_tile = lax.dynamic_slice_in_dim(prototype_normalized, block_index * C_DEV, C_DEV, 1)
        logits = jnp.dot(s_hat, centroid_tile, preferred_element_type=jnp.float32) / 0.1
        return (carried + lax.optimization_barrier(jnp.sum(jnp.exp(logits), axis=1)), None)
    totals, unused = lax.scan(total_step, jnp.zeros((MASKED,), jnp.float32), block_ids)

    def grad_step(carried, block_index):
        cross_term, feat_grad = carried
        centroid_tile = lax.dynamic_slice_in_dim(prototype_normalized, block_index * C_DEV, C_DEV, 1)
        eblock = teacher_block(block_index)
        ablock = lax.dynamic_slice_in_dim(row_factor, block_index * C_DEV, C_DEV, 0)
        logits = jnp.dot(s_hat, centroid_tile, preferred_element_type=jnp.float32) / 0.1
        goal_distribution = eblock * ablock[None, :] * column_factor[:, None]
        cross_term = cross_term + lax.optimization_barrier(jnp.sum(goal_distribution * logits, axis=1))
        logit_grad = ((jnp.exp(logits) / totals[:, None] - goal_distribution) / (0.1 * MASKED)).astype(jnp.bfloat16)
        feat_grad = feat_grad + jnp.dot(logit_grad, centroid_tile.T, preferred_element_type=jnp.float32)
        dwblock = jnp.dot(s_hat.T, logit_grad, preferred_element_type=jnp.float32)
        return ((cross_term, feat_grad), dwblock)
    initial = (jnp.zeros((MASKED,), jnp.float32), jnp.zeros((MASKED, K), jnp.float32))
    (cross_term, feat_grad), dwblocks = lax.scan(grad_step, initial, block_ids)
    patch_loss = jnp.log(totals) - cross_term
    dw_hat = jnp.transpose(dwblocks, (1, 0, 2)).reshape(K, PROTOS)
    grad_student = pull_s(feat_grad)[0]
    grad_protos = pull_w(dw_hat)[0]
    return (patch_loss, grad_student, grad_protos)
```

```python
import functools

import jax
import jax.numpy as jnp
from jax import lax
from jax.experimental import pallas as pl
from jax.experimental.pallas import tpu as pltpu
from jax.sharding import PartitionSpec as P

ITERS = 3
HEATUP_LENGTH = 30
MESH = pl.DeviceIdType.MESH
F32 = jnp.float32
BF16 = jnp.bfloat16
U_T, U_S, U_P, U_G = 4, 2, 8, 4
VLIM = 62
NT = (((1,), (1,)), ((), ()))


def diagonal(size):
    return lax.broadcasted_iota(jnp.int32, (size, size), 0) == lax.broadcasted_iota(
        jnp.int32, (size, size), 1
    )


def to_row(column, eye):
    return jnp.sum(jnp.where(eye, column, 0.0), axis=0, keepdims=True)


def to_column(row, eye):
    return jnp.sum(jnp.where(eye, row, 0.0), axis=1, keepdims=True)


def remote(src, dst, send, recv, axis, peer):
    return pltpu.make_async_remote_copy(
        src_ref=src,
        dst_ref=dst,
        send_sem=send,
        recv_sem=recv,
        device_id={axis: peer},
        device_id_type=MESH,
    )


def await_bytes(ref, sem):
    pltpu.make_async_copy(ref, ref, sem).wait()


def kernel(
    n_proto,
    n_patch,
    progress_hbm,
    teacher_hbm,
    student_hbm,
    masked_hbm,
    proto_hbm,
    loss_ref,
    gs_ref,
    gp_ref,
    progress_ref,
    teacher_ref,
    student_ref,
    masked_ref,
    proto_ref,
    rw_ref,
    load_sem,
    w_hat,
    e_ref,
    s_ref,
    p_ref,
    g_ref,
    rows_ref,
    shat_t,
    ds_ref,
    dw_ref,
    col_buf,
    row_buf,
    last_buf,
    feat_one,
    feat_two,
    w_one,
    w_two,
    col_send,
    col_recv,
    row_send,
    row_recv,
    feat_one_send,
    feat_one_recv,
    feat_two_sem,
    w_sem,
):
    me_p = lax.axis_index("proto")
    me_q = lax.axis_index("patch")
    images, slots = masked_ref.shape
    per_image = teacher_ref.shape[0] // images
    width, cols = proto_ref.shape
    rows = images * slots
    chunk = cols // 4

    loads = [
        pltpu.make_async_copy(src, dst, load_sem.at[k])
        for k, (src, dst) in enumerate(
            (
                (proto_hbm, proto_ref),
                (masked_hbm, masked_ref),
                (teacher_hbm, teacher_ref),
                (student_hbm, student_ref),
                (progress_hbm, progress_ref),
            )
        )
    ]
    for load in loads:
        load.start()

    barrier = pltpu.get_barrier_semaphore()

    def greet(axis, me, n):
        def body(d, carry):
            pl.semaphore_signal(
                barrier, inc=1, device_id={axis: lax.rem(me + d, n)}, device_id_type=MESH
            )
            return carry

        lax.fori_loop(1, n, body, 0)

    greet("proto", me_p, n_proto)
    greet("patch", me_q, n_patch)

    eye = diagonal(slots)
    lane = lax.broadcasted_iota(jnp.int32, (slots, slots), 1)

    def block(i):
        return pl.ds(pl.multiple_of(i * slots, slots), slots)

    def gathered(ref, i):
        picks = masked_ref[pl.ds(i, 1), :]
        picks = jnp.sum(jnp.where(eye, picks, 0), axis=1, keepdims=True)
        out = None
        for part in range(per_image // slots):
            hot = jnp.where(picks == lane + part * slots, 1.0, 0.0).astype(BF16)
            base = pl.multiple_of(i * per_image + part * slots, slots)
            term = jnp.dot(hot, ref[pl.ds(base, slots), :], preferred_element_type=F32)
            out = term if out is None else out + term
        return out

    def unit(x):
        return x * lax.rsqrt(jnp.sum(x * x, axis=1, keepdims=True) + 1e-12)

    def folded(x):
        return jnp.sum(x.reshape(slots // 8, 8, cols), axis=0)

    loads[0].wait()
    w_raw = proto_ref[...].astype(F32)
    r_w = lax.rsqrt(jnp.sum(w_raw * w_raw, axis=0, keepdims=True) + 1e-12)
    rw_ref[...] = r_w
    w_hat[...] = (w_raw * r_w).astype(BF16)

    loads[4].wait()
    steps = jnp.broadcast_to(progress_ref[...].astype(F32), (1, cols))
    sharpness = 1.0 / (0.04 + 0.03 * steps / HEATUP_LENGTH)

    def teacher_block(i, acc):
        t_hat = unit(gathered(teacher_ref, i)).astype(BF16)
        e = jnp.exp(jnp.dot(t_hat, w_hat[...], preferred_element_type=F32) * sharpness)
        e_ref[block(i), :] = e
        return acc + folded(e)

    def student_block(i, carry):
        x = gathered(student_ref, i)
        rows_ref[block(i), :] = x
        s_hat = unit(x)
        shat_t[:, block(i)] = s_hat.T.astype(BF16)
        s = jnp.dot(s_hat.astype(BF16), w_hat[...], preferred_element_type=F32) / 0.1
        s_ref[block(i), :] = s
        p = jnp.exp(s)
        p_ref[block(i), :] = p
        total = jnp.sum(p, axis=1, keepdims=True)
        at = pl.ds(pl.multiple_of(2 * rows + i * slots, slots), slots)
        last_buf[me_p, :, at] = to_row(total, eye)
        return carry

    def send_all(buf, axis, me, n, send, recv):
        def body(d, carry):
            remote(buf.at[me], buf.at[me], send, recv, axis, lax.rem(me + d, n)).start()
            return carry

        lax.fori_loop(1, n, body, 0)

    def wait_all(buf, n, send, recv):
        await_bytes(buf.at[pl.ds(0, n - 1)], recv)
        await_bytes(buf.at[pl.ds(0, n - 1)], send)

    def column_pass(b_row_at, acc0):
        def body(i, acc):
            b_col = to_column(b_row_at(i), eye)
            return acc + folded(e_ref[block(i), :] * b_col)

        return lax.fori_loop(0, images, body, acc0, unroll=U_P)

    share = images // 4
    zero = jnp.zeros((8, cols), F32)
    loads[1].wait()
    loads[2].wait()
    acc = lax.fori_loop(0, images, teacher_block, zero, unroll=U_T)
    loads[3].wait()
    pl.semaphore_wait(barrier, n_proto + n_patch - 2)
    for it in range(ITERS):
        col_buf[it, me_q, :, :] = jnp.sum(acc, axis=0, keepdims=True)
        send_all(
            col_buf.at[it], "patch", me_q, n_patch, col_send.at[it], col_recv.at[it]
        )
        if it < 2:
            lax.fori_loop(2 * it * share, (2 * it + 1) * share, student_block, 0, unroll=U_S)
        wait_all(col_buf.at[it], n_patch, col_send.at[it], col_recv.at[it])
        a_row = 1.0 / jnp.sum(col_buf[it], axis=0)

        if it + 1 < ITERS:

            def row_body(i, carry):
                r = jnp.sum(e_ref[block(i), :] * a_row, axis=1, keepdims=True)
                row_buf[it, me_p, :, block(i)] = to_row(r, eye)
                return carry

            lax.fori_loop(0, images, row_body, 0, unroll=U_P)
            buf = row_buf.at[it]
            send_all(buf, "proto", me_p, n_proto, row_send.at[it], row_recv.at[it])
            first, stop = (2 * it + 1) * share, (2 * it + 2) * share
            lax.fori_loop(first, images if it == 1 else stop, student_block, 0, unroll=U_S)
            wait_all(buf, n_proto, row_send.at[it], row_recv.at[it])
            b_rows = 1.0 / jnp.sum(row_buf[it], axis=0)
            loss_ref[...] = b_rows
            acc = column_pass(lambda i: loss_ref[:, block(i)], zero)

    def last_body(i, carry):
        ea = e_ref[block(i), :] * a_row
        e_ref[block(i), :] = ea
        r = jnp.sum(ea, axis=1, keepdims=True)
        x = jnp.sum(ea * s_ref[block(i), :], axis=1, keepdims=True)
        last_buf[me_p, :, block(i)] = to_row(r, eye)
        last_buf[me_p, :, pl.ds(pl.multiple_of(rows + i * slots, slots), slots)] = (
            to_row(x, eye)
        )
        return carry

    lax.fori_loop(0, images, last_body, 0, unroll=U_P)
    send_all(last_buf, "proto", me_p, n_proto, row_send.at[2], row_recv.at[2])
    wait_all(last_buf, n_proto, row_send.at[2], row_recv.at[2])
    sums = jnp.sum(last_buf[...], axis=0)
    b_row = 1.0 / sums[:, :rows]
    totals = sums[:, 2 * rows :]
    loss_ref[...] = jnp.log(totals) - sums[:, rows : 2 * rows] * b_row
    scale = 1.0 / (0.1 * rows * n_patch)
    col_buf[0, 0, :, :] = b_row * scale
    col_buf[0, 1, :, :] = scale / totals

    half = n_proto // 2
    hi, lo = me_p // 2, lax.rem(me_p, 2)
    other = 1 - lo
    piece = rows // n_proto
    per_block = n_proto // images

    def part(ref, o, size):
        return ref.at[pl.ds(pl.multiple_of(o * size, size), size), :]

    def to_pair(o_hi):
        src = part(ds_ref, o_hi * 2 + other, piece)
        remote(
            src,
            feat_one.at[o_hi],
            feat_one_send,
            feat_one_recv.at[o_hi],
            "proto",
            hi * 2 + other,
        ).start()

    upper = (2 * hi) // half

    def far_first(j):
        down = half - 1 - j - (j + hi + 1) // half
        up = j + (j + half - hi) // half
        return (1 - upper) * down + upper * up

    def grad_block(i):
        b_col = to_column(col_buf[0, 0, :, block(i)], eye)
        t_col = to_column(col_buf[0, 1, :, block(i)], eye)
        g = (p_ref[block(i), :] * t_col - e_ref[block(i), :] * b_col).astype(BF16)
        g_ref[block(i), :] = g
        ds_ref[block(i), :] = lax.dot_general(g, w_hat[...], NT, preferred_element_type=F32)

    def send_far(j, carry):
        to_pair(far_first(j))
        return carry

    def first_half(j, carry):
        o_hi = far_first(j)
        grad_block(2 * o_hi + other)
        to_pair(o_hi)
        return carry

    def second_half(j, carry):
        grad_block(2 * j + lo)
        return carry

    def any_block(j, carry):
        grad_block(j)
        return carry

    if per_block == 1:
        lax.fori_loop(0, half - 1, first_half, 0)
        grad_block(2 * hi + other)
        to_pair(hi)
        lax.fori_loop(0, half, second_half, 0, unroll=U_G)
    else:
        lax.fori_loop(0, images, any_block, 0, unroll=U_G)
        lax.fori_loop(0, half - 1, send_far, 0)
        to_pair(hi)

    def dw_body(j, carry):
        at = pl.ds(pl.multiple_of(j * chunk, chunk), chunk)
        dw = jnp.dot(shat_t[...], g_ref[:, at], preferred_element_type=F32)
        dw_ref[:, at] = dw
        col_buf[ITERS, me_q, :, at] = jnp.sum(
            dw * proto_ref[:, at].astype(F32), axis=0, keepdims=True
        )
        return carry

    lax.fori_loop(0, cols // chunk, dw_body, 0)
    k_piece = width // n_patch
    q_half = n_patch // 2
    q_hi, q_lo = me_q // 2, lax.rem(me_q, 2)
    q_other = 1 - q_lo

    def w_pair(o_hi, carry):
        remote(
            part(dw_ref, o_hi * 2 + q_other, k_piece),
            w_one.at[o_hi],
            w_sem.at[0],
            w_sem.at[1],
            "patch",
            q_hi * 2 + q_other,
        ).start()
        return carry

    lax.fori_loop(0, q_half, w_pair, 0)
    dots = col_buf.at[ITERS]
    send_all(dots, "patch", me_q, n_patch, col_send.at[ITERS], col_recv.at[ITERS])
    def feat_add(o_hi):
        await_bytes(feat_one.at[o_hi], feat_one_recv.at[o_hi])
        return part(ds_ref, o_hi * 2 + lo, piece)[...] + feat_one[o_hi]

    def feat_rest(j, carry):
        o_hi = far_first(j)
        mine = part(ds_ref, o_hi * 2 + lo, piece)
        mine[...] = feat_add(o_hi)
        remote(
            mine,
            feat_two.at[hi],
            feat_two_sem.at[0],
            feat_two_sem.at[1],
            "proto",
            o_hi * 2 + lo,
        ).start()
        return carry

    feat_rest(0, 0)
    await_bytes(w_one, w_sem.at[1])

    def w_rest(d, carry):
        o_hi = lax.rem(q_hi + d, q_half)
        mine = part(dw_ref, o_hi * 2 + q_lo, k_piece)
        mine[...] = mine[...] + w_one[o_hi]
        remote(
            mine, w_two.at[q_hi], w_sem.at[2], w_sem.at[3], "patch", o_hi * 2 + q_lo
        ).start()
        return carry

    lax.fori_loop(1, q_half, w_rest, 0)
    w_two[q_hi, :, :] = part(dw_ref, me_q, k_piece)[...] + w_one[q_hi]

    lax.fori_loop(1, half - 1, feat_rest, 0)
    feat_two[hi, :, :] = feat_add(hi)

    wait_all(dots, n_patch, col_send.at[ITERS], col_recv.at[ITERS])
    await_bytes(w_two.at[pl.ds(0, q_half - 1)], w_sem.at[3])
    dot = jnp.sum(col_buf[ITERS], axis=0)
    r_w = rw_ref[...]
    w_mine = part(proto_ref, me_q, k_piece)[...].astype(F32)
    gp_ref[...] = r_w * jnp.sum(w_two[...], axis=0) - w_mine * (r_w * r_w * r_w * dot)

    await_bytes(feat_two.at[pl.ds(0, half - 1)], feat_two_sem.at[1])
    x = part(rows_ref, me_p, piece)[...]
    g = jnp.sum(feat_two[...], axis=0)
    r = lax.rsqrt(jnp.sum(x * x, axis=1, keepdims=True) + 1e-12)
    gs_ref[...] = r * g - x * (r * r * r * jnp.sum(x * g, axis=1, keepdims=True))

    await_bytes(w_one, w_sem.at[0])
    await_bytes(w_two.at[pl.ds(0, q_half - 1)], w_sem.at[2])
    await_bytes(feat_one, feat_one_send)
    await_bytes(feat_two.at[pl.ds(0, half - 1)], feat_two_sem.at[0])


def finish(loss_in, gs_in, gp_in, loss_ref, gs_ref, gp_ref):
    loss_ref[...] = loss_in[...].reshape(loss_ref.shape)
    gs_ref[...] = gs_in[...]
    gp_ref[...] = gp_in[...]


def solution(mesh):
    n_proto, n_patch = mesh.shape["proto"], mesh.shape["patch"]

    def shards(teacher_feats, student_feats, masked, progress_counter, prototypes):
        images, slots = masked.shape
        rows = images * slots
        width, cols = prototypes.shape
        piece, k_piece = rows // n_proto, width // n_patch
        vmem = pl.BlockSpec(memory_space=pltpu.VMEM)
        held = pl.pallas_call(
            functools.partial(kernel, n_proto, n_patch),
            out_shape=(
                pltpu.VMEM((1, rows), F32),
                pltpu.VMEM((piece, width), F32),
                pltpu.VMEM((k_piece, cols), F32),
            ),
            in_specs=[pl.BlockSpec(memory_space=pltpu.HBM)] * 5,
            out_specs=(vmem, vmem, vmem),
            scratch_shapes=[
                pltpu.VMEM((1, 1), jnp.int32),
                pltpu.VMEM(teacher_feats.shape, BF16),
                pltpu.VMEM(student_feats.shape, BF16),
                pltpu.VMEM(masked.shape, jnp.int32),
                pltpu.VMEM(prototypes.shape, BF16),
                pltpu.VMEM((1, cols), F32),
                pltpu.SemaphoreType.DMA((5,)),
                pltpu.VMEM((width, cols), BF16),
                pltpu.VMEM((rows, cols), F32),
                pltpu.VMEM((rows, cols), F32),
                pltpu.VMEM((rows, cols), F32),
                pltpu.VMEM((rows, cols), BF16),
                pltpu.VMEM((rows, width), F32),
                pltpu.VMEM((width, rows), BF16),
                pltpu.VMEM((rows, width), F32),
                pltpu.VMEM((width, cols), F32),
                pltpu.VMEM((ITERS + 1, n_patch, 1, cols), F32),
                pltpu.VMEM((ITERS - 1, n_proto, 1, rows), F32),
                pltpu.VMEM((n_proto, 1, 3 * rows), F32),
                pltpu.VMEM((n_proto // 2, piece, width), F32),
                pltpu.VMEM((n_proto // 2, piece, width), F32),
                pltpu.VMEM((n_patch // 2, k_piece, cols), F32),
                pltpu.VMEM((n_patch // 2, k_piece, cols), F32),
                pltpu.SemaphoreType.DMA((ITERS + 1,)),
                pltpu.SemaphoreType.DMA((ITERS + 1,)),
                pltpu.SemaphoreType.DMA((ITERS,)),
                pltpu.SemaphoreType.DMA((ITERS,)),
                pltpu.SemaphoreType.DMA,
                pltpu.SemaphoreType.DMA((n_proto // 2,)),
                pltpu.SemaphoreType.DMA((2,)),
                pltpu.SemaphoreType.DMA((4,)),
            ],
            compiler_params=pltpu.CompilerParams(
                collective_id=0, has_side_effects=True, vmem_limit_bytes=VLIM << 20
            ),
        )(progress_counter.reshape(1, 1), teacher_feats, student_feats, masked, prototypes)
        return tuple(
            pl.pallas_call(
                finish,
                out_shape=(
                    jax.ShapeDtypeStruct((rows,), F32),
                    jax.ShapeDtypeStruct((piece, width), F32),
                    jax.ShapeDtypeStruct((k_piece, cols), F32),
                ),
                in_specs=[vmem] * 3,
                out_specs=(vmem,) * 3,
            )(*(pltpu.with_memory_space_constraint(x, pltpu.VMEM) for x in held))
        )

    in_specs = (P("patch", None), P("patch", None), P("patch", None), P(), P(None, "proto"))
    out_specs = (P("patch"), P(("patch", "proto"), None), P("patch", "proto"))
    return jax.shard_map(shards, mesh=mesh, in_specs=in_specs, out_specs=out_specs, check_vma=False)
```

```python
import functools

import jax
import jax.numpy as jnp
from jax import lax
from jax.experimental import pallas as pl
from jax.experimental.pallas import tpu as pltpu
from jax.sharding import PartitionSpec as P

ITERS = 3
HEATUP_LENGTH = 30
LOG2E = 1.4426950408889634
MESH = pl.DeviceIdType.MESH
F32 = jnp.float32
BF16 = jnp.bfloat16
U_T, U_S, U_P, U_G = 4, 2, 8, 4
TILE, RB = 256, 256
TOTAL, CROSS = ITERS, ITERS + 1
VLIM = 62
NT = (((1,), (1,)), ((), ()))


def diagonal(size):
    return lax.broadcasted_iota(jnp.int32, (size, size), 0) == lax.broadcasted_iota(
        jnp.int32, (size, size), 1
    )


def to_row(column, eye):
    return jnp.sum(jnp.where(eye, column, 0.0), axis=0, keepdims=True)


def to_column(row, eye):
    return jnp.sum(jnp.where(eye, row, 0.0), axis=1, keepdims=True)


def remote(src, dst, send, recv, axis, peer):
    return pltpu.make_async_remote_copy(
        src_ref=src,
        dst_ref=dst,
        send_sem=send,
        recv_sem=recv,
        device_id={axis: peer},
        device_id_type=MESH,
    )


def await_bytes(ref, sem):
    pltpu.make_async_copy(ref, ref, sem).wait()


def kernel(
    n_proto,
    n_patch,
    progress_hbm,
    teacher_hbm,
    student_hbm,
    masked_hbm,
    proto_hbm,
    loss_ref,
    gs_ref,
    gp_ref,
    progress_ref,
    teacher_ref,
    student_ref,
    masked_ref,
    proto_ref,
    rw_ref,
    load_sem,
    w_hat,
    e_ref,
    s_ref,
    p_ref,
    g_ref,
    rows_ref,
    shat_t,
    ds_ref,
    dw_ref,
    t_hat,
    s_hat,
    sharp_ref,
    da_ref,
    t_ref,
    b_ref,
    feat_zero,
    feat_zero_sem,
    col_buf,
    row_buf,
    feat_one,
    feat_two,
    w_one,
    w_two,
    col_send,
    col_recv,
    row_send,
    row_recv,
    feat_one_send,
    feat_one_recv,
    feat_two_sem,
    w_sem,
):
    me_p = lax.axis_index("proto")
    me_q = lax.axis_index("patch")
    images, slots = masked_ref.shape
    per_image = teacher_ref.shape[0] // images
    width, cols = proto_ref.shape
    rows = images * slots
    chunk = cols // 4

    loads = [
        pltpu.make_async_copy(src, dst, load_sem.at[k])
        for k, (src, dst) in enumerate(
            (
                (proto_hbm, proto_ref),
                (masked_hbm, masked_ref),
                (progress_hbm, progress_ref),
                (teacher_hbm, teacher_ref),
                (student_hbm, student_ref),
            )
        )
    ]
    for load in loads:
        load.start()

    barrier = pltpu.get_barrier_semaphore()

    def greet(axis, me, n):
        def body(d, carry):
            pl.semaphore_signal(
                barrier, inc=1, device_id={axis: lax.rem(me + d, n)}, device_id_type=MESH
            )
            return carry

        lax.fori_loop(1, n, body, 0)

    greet("proto", me_p, n_proto)
    greet("patch", me_q, n_patch)

    eye = diagonal(slots)
    lane = lax.broadcasted_iota(jnp.int32, (slots, per_image), 1)

    def block(i):
        return pl.ds(pl.multiple_of(i * slots, slots), slots)

    def gathered(ref, i):
        picks = masked_ref[pl.ds(i, 1), :]
        picks = jnp.sum(jnp.where(eye, picks, 0), axis=1, keepdims=True)
        hot = jnp.where(picks == lane, 1.0, 0.0).astype(BF16)
        at = pl.ds(pl.multiple_of(i * per_image, per_image), per_image)
        return jnp.dot(hot, ref[at, :], preferred_element_type=F32)

    def unit(x):
        return x * lax.rsqrt(jnp.sum(x * x, axis=1, keepdims=True) + 1e-12)

    def folded(x):
        return jnp.sum(x.reshape(slots // 8, 8, cols), axis=0)

    loads[0].wait()
    w_raw = proto_ref[...].astype(F32)
    r_w = lax.rsqrt(jnp.sum(w_raw * w_raw, axis=0, keepdims=True) + 1e-12)
    rw_ref[...] = r_w
    w_hat[...] = (w_raw * r_w).astype(BF16)

    loads[2].wait()
    steps = jnp.broadcast_to(progress_ref[...].astype(F32), (1, cols))
    sharp_ref[...] = LOG2E / (0.04 + 0.03 * steps / HEATUP_LENGTH)

    def teacher_rows(i, carry):
        t_hat[block(i), :] = unit(gathered(teacher_ref, i)).astype(BF16)
        return carry

    def teacher_tile(j, carry):
        at = pl.ds(pl.multiple_of(j * TILE, TILE), TILE)
        total = None
        for k in range(rows // RB):
            here = pl.ds(k * RB, RB)
            e = jnp.dot(t_hat[here, :], w_hat[:, at], preferred_element_type=F32)
            e = jnp.exp2(e * sharp_ref[:, at])
            e_ref[here, at] = e
            part_sum = jnp.sum(e.reshape(RB // 8, 8, TILE), axis=0)
            total = part_sum if total is None else total + part_sum
        col_buf[0, me_q, :, at] = jnp.sum(total, axis=0, keepdims=True)
        return carry

    def student_rows(i, carry):
        x = gathered(student_ref, i)
        rows_ref[block(i), :] = x
        s_unit = unit(x)
        s_hat[block(i), :] = s_unit.astype(BF16)
        shat_t[:, block(i)] = s_unit.T.astype(BF16)
        return carry

    def student_block(i, carry):
        s = jnp.dot(s_hat[block(i), :], w_hat[...], preferred_element_type=F32)
        s_ref[block(i), :] = s
        p = jnp.exp2(s * (10.0 * LOG2E))
        p_ref[block(i), :] = p
        total = jnp.sum(p, axis=1, keepdims=True)
        row_buf[TOTAL, me_p, :, block(i)] = to_row(total, eye)
        return carry

    def spread(x):
        high = x.astype(BF16)
        low = (x - high.astype(F32)).astype(BF16)
        w = w_hat[...]
        return lax.dot_general(high, w, NT, preferred_element_type=F32) + lax.dot_general(
            low, w, NT, preferred_element_type=F32
        )

    def a_block(i, carry):
        da_ref[block(i), :] = spread(p_ref[block(i), :])
        return carry

    def b_block(i, carry):
        ds_ref[block(i), :] = spread(e_ref[block(i), :])
        return carry

    def send_all(buf, axis, me, n, send, recv):
        def body(d, carry):
            remote(buf.at[me], buf.at[me], send, recv, axis, lax.rem(me + d, n)).start()
            return carry

        lax.fori_loop(1, n, body, 0)

    def wait_all(buf, n, send, recv):
        await_bytes(buf.at[pl.ds(0, n - 1)], recv)
        await_bytes(buf.at[pl.ds(0, n - 1)], send)

    def column_pass(b_row_at, acc0):
        def body(i, acc):
            b_col = to_column(b_row_at(i), eye)
            return acc + folded(e_ref[block(i), :] * b_col)

        return lax.fori_loop(0, images, body, acc0, unroll=U_P)

    half = n_proto // 2
    hi, lo = me_p // 2, lax.rem(me_p, 2)
    other = 1 - lo
    piece = rows // n_proto
    whole_blocks = n_proto == images
    upper = (2 * hi) // half

    def far_first(j):
        down = half - 1 - j - (j + hi + 1) // half
        up = j + (j + half - hi) // half
        return (1 - upper) * down + upper * up

    def place(j):
        return far_first(j) if j < half - 1 else hi

    def part(ref, o, size):
        return ref.at[pl.ds(pl.multiple_of(o * size, size), size), :]

    def a_pair(o_hi):
        remote(
            part(da_ref, o_hi * 2 + other, piece),
            feat_zero.at[o_hi],
            feat_zero_sem.at[0],
            feat_zero_sem.at[1],
            "proto",
            hi * 2 + other,
        ).start()

    def b_pair(o_hi):
        remote(
            part(ds_ref, o_hi * 2 + other, piece),
            feat_one.at[o_hi],
            feat_one_send,
            feat_one_recv.at[o_hi],
            "proto",
            hi * 2 + other,
        ).start()

    def each(n, f):
        def body(j, carry):
            f(j)
            return carry

        lax.fori_loop(0, n, body, 0)

    zero = jnp.zeros((8, cols), F32)
    loads[1].wait()
    loads[3].wait()
    lax.fori_loop(0, images, teacher_rows, 0, unroll=True)
    lax.fori_loop(0, cols // TILE, teacher_tile, 0, unroll=U_T)
    loads[4].wait()
    pl.semaphore_wait(barrier, n_proto + n_patch - 2)

    def send_rows(k):
        send_all(row_buf.at[k], "proto", me_p, n_proto, row_send.at[k], row_recv.at[k])

    def wait_rows(k):
        wait_all(row_buf.at[k], n_proto, row_send.at[k], row_recv.at[k])

    def send_cols(k):
        send_all(col_buf.at[k], "patch", me_q, n_patch, col_send.at[k], col_recv.at[k])

    def wait_cols(k):
        wait_all(col_buf.at[k], n_patch, col_send.at[k], col_recv.at[k])

    def row_pass(it):
        a_row = 1.0 / jnp.sum(col_buf[it], axis=0)

        def body(i, carry):
            ea = e_ref[block(i), :] * a_row
            if it + 1 == ITERS:
                e_ref[block(i), :] = ea
            row_buf[it, me_p, :, block(i)] = to_row(jnp.sum(ea, axis=1, keepdims=True), eye)
            return carry

        lax.fori_loop(0, images, body, 0, unroll=U_P)
        send_rows(it)

    def col_pass(it):
        loss_ref[...] = 1.0 / jnp.sum(row_buf[it], axis=0)
        acc = column_pass(lambda i: loss_ref[:, block(i)], zero)
        col_buf[it + 1, me_q, :, :] = jnp.sum(acc, axis=0, keepdims=True)
        send_cols(it + 1)

    send_cols(0)
    lax.fori_loop(0, images, student_rows, 0, unroll=U_S)
    if whole_blocks:
        student_block(2 * place(0) + other, 0)
    wait_cols(0)

    row_pass(0)
    if whole_blocks:
        a_block(2 * place(0) + other, 0)
        a_pair(place(0))
        student_block(2 * place(1) + other, 0)
        a_block(2 * place(1) + other, 0)
        a_pair(place(1))
        for j in range(2, half):
            student_block(2 * place(j) + other, 0)
        student_block(lo, 0)
    else:
        lax.fori_loop(0, images, student_block, 0, unroll=U_S)
    wait_rows(0)
    col_pass(0)
    if whole_blocks:
        for j in range(1, half):
            student_block(2 * j + lo, 0)
    wait_cols(1)

    row_pass(1)
    send_rows(TOTAL)
    if whole_blocks:
        for j in range(2, half):
            a_block(2 * place(j) + other, 0)
            a_pair(place(j))
        for j in range(half):
            a_block(2 * j + lo, 0)
    else:
        lax.fori_loop(0, images, a_block, 0, unroll=U_S)
        each(half, a_pair)
    wait_rows(1)
    col_pass(1)

    wait_rows(TOTAL)
    totals = jnp.sum(row_buf[TOTAL], axis=0)
    scale = 1.0 / (0.1 * rows * n_patch)
    col_buf[0, 1, :, :] = scale / totals

    def weigh(i, carry):
        t_col = to_column(col_buf[0, 1, :, block(i)], eye)
        t_ref[block(i), :] = t_col
        p_ref[block(i), :] = p_ref[block(i), :] * t_col
        return carry

    lax.fori_loop(0, images, weigh, 0, unroll=U_S)
    await_bytes(feat_zero, feat_zero_sem.at[1])

    def join(g):
        mine = part(da_ref, 2 * g + lo, piece)
        mine[...] = (mine[...] + feat_zero[g]) * part(t_ref, 2 * g + lo, piece)[...]

    each(half, join)
    wait_cols(2)

    row_pass(2)

    def cross_body(i, carry):
        x = jnp.sum(e_ref[block(i), :] * s_ref[block(i), :], axis=1, keepdims=True)
        row_buf[CROSS, me_p, :, block(i)] = to_row(x, eye)
        return carry

    def cross():
        lax.fori_loop(0, images, cross_body, 0, unroll=U_S)
        send_rows(CROSS)

    if whole_blocks:
        for j in range(half):
            b_block(2 * place(j) + other, 0)
            b_pair(place(j))
            if j == 0:
                cross()
        for j in range(half):
            b_block(2 * j + lo, 0)
    else:
        lax.fori_loop(0, images, b_block, 0, unroll=U_S)
        cross()
        each(half, b_pair)

    wait_rows(2)
    b_row = 1.0 / jnp.sum(row_buf[2], axis=0)
    col_buf[0, 0, :, :] = b_row * scale

    def to_b(i, carry):
        b_ref[block(i), :] = to_column(col_buf[0, 0, :, block(i)], eye)
        return carry

    lax.fori_loop(0, images, to_b, 0, unroll=U_P)

    def feat_add(o_hi):
        await_bytes(feat_one.at[o_hi], feat_one_recv.at[o_hi])
        o = o_hi * 2 + lo
        both = part(ds_ref, o, piece)[...] + feat_one[o_hi]
        return part(da_ref, o, piece)[...] - part(b_ref, o, piece)[...] * both

    def feat_rest(j, carry):
        o_hi = far_first(j)
        mine = part(da_ref, o_hi * 2 + lo, piece)
        mine[...] = feat_add(o_hi)
        remote(
            mine,
            feat_two.at[hi],
            feat_two_sem.at[0],
            feat_two_sem.at[1],
            "proto",
            o_hi * 2 + lo,
        ).start()
        return carry

    feat_rest(0, 0)

    def g_block(i, carry):
        g = p_ref[block(i), :] - e_ref[block(i), :] * b_ref[block(i), :]
        g_ref[block(i), :] = g.astype(BF16)
        return carry

    lax.fori_loop(0, images, g_block, 0, unroll=U_G)

    def dw_body(j, carry):
        at = pl.ds(pl.multiple_of(j * chunk, chunk), chunk)
        dw = jnp.dot(shat_t[...], g_ref[:, at], preferred_element_type=F32)
        dw_ref[:, at] = dw
        col_buf[ITERS, me_q, :, at] = jnp.sum(
            dw * proto_ref[:, at].astype(F32), axis=0, keepdims=True
        )
        return carry

    lax.fori_loop(0, cols // chunk, dw_body, 0)
    k_piece = width // n_patch
    q_half = n_patch // 2
    q_hi, q_lo = me_q // 2, lax.rem(me_q, 2)
    q_other = 1 - q_lo

    def w_pair(o_hi, carry):
        remote(
            part(dw_ref, o_hi * 2 + q_other, k_piece),
            w_one.at[o_hi],
            w_sem.at[0],
            w_sem.at[1],
            "patch",
            q_hi * 2 + q_other,
        ).start()
        return carry

    lax.fori_loop(0, q_half, w_pair, 0)
    dots = col_buf.at[ITERS]
    send_all(dots, "patch", me_q, n_patch, col_send.at[ITERS], col_recv.at[ITERS])
    feat_rest(1, 0)
    await_bytes(w_one, w_sem.at[1])

    def w_rest(d, carry):
        o_hi = lax.rem(q_hi + d, q_half)
        mine = part(dw_ref, o_hi * 2 + q_lo, k_piece)
        mine[...] = mine[...] + w_one[o_hi]
        remote(
            mine, w_two.at[q_hi], w_sem.at[2], w_sem.at[3], "patch", o_hi * 2 + q_lo
        ).start()
        return carry

    lax.fori_loop(1, q_half, w_rest, 0)
    w_two[q_hi, :, :] = part(dw_ref, me_q, k_piece)[...] + w_one[q_hi]

    lax.fori_loop(2, half - 1, feat_rest, 0)
    feat_two[hi, :, :] = feat_add(hi)

    wait_all(dots, n_patch, col_send.at[ITERS], col_recv.at[ITERS])
    await_bytes(w_two.at[pl.ds(0, q_half - 1)], w_sem.at[3])
    wait_rows(CROSS)
    loss_ref[...] = jnp.log(totals) - 10.0 * jnp.sum(row_buf[CROSS], axis=0) * b_row
    dot = jnp.sum(col_buf[ITERS], axis=0)
    r_w = rw_ref[...]
    w_mine = part(proto_ref, me_q, k_piece)[...].astype(F32)
    gp_ref[...] = r_w * jnp.sum(w_two[...], axis=0) - w_mine * (r_w * r_w * r_w * dot)

    await_bytes(feat_two.at[pl.ds(0, half - 1)], feat_two_sem.at[1])
    x = part(rows_ref, me_p, piece)[...]
    g = jnp.sum(feat_two[...], axis=0)
    r = lax.rsqrt(jnp.sum(x * x, axis=1, keepdims=True) + 1e-12)
    gs_ref[...] = r * g - x * (r * r * r * jnp.sum(x * g, axis=1, keepdims=True))

    await_bytes(w_one, w_sem.at[0])
    await_bytes(w_two.at[pl.ds(0, q_half - 1)], w_sem.at[2])
    await_bytes(feat_zero, feat_zero_sem.at[0])
    await_bytes(feat_one, feat_one_send)
    await_bytes(feat_two.at[pl.ds(0, half - 1)], feat_two_sem.at[0])


def finish(loss_in, gs_in, gp_in, loss_ref, gs_ref, gp_ref):
    loss_ref[...] = loss_in[...].reshape(loss_ref.shape)
    gs_ref[...] = gs_in[...]
    gp_ref[...] = gp_in[...]


def solution(mesh):
    n_proto, n_patch = mesh.shape["proto"], mesh.shape["patch"]

    def shards(teacher_feats, student_feats, masked, progress_counter, prototypes):
        images, slots = masked.shape
        rows = images * slots
        width, cols = prototypes.shape
        piece, k_piece = rows // n_proto, width // n_patch
        vmem = pl.BlockSpec(memory_space=pltpu.VMEM)
        held = pl.pallas_call(
            functools.partial(kernel, n_proto, n_patch),
            out_shape=(
                pltpu.VMEM((1, rows), F32),
                pltpu.VMEM((piece, width), F32),
                pltpu.VMEM((k_piece, cols), F32),
            ),
            in_specs=[pl.BlockSpec(memory_space=pltpu.HBM)] * 5,
            out_specs=(vmem, vmem, vmem),
            scratch_shapes=[
                pltpu.VMEM((1, 1), jnp.int32),
                pltpu.VMEM(teacher_feats.shape, BF16),
                pltpu.VMEM(student_feats.shape, BF16),
                pltpu.VMEM(masked.shape, jnp.int32),
                pltpu.VMEM(prototypes.shape, BF16),
                pltpu.VMEM((1, cols), F32),
                pltpu.SemaphoreType.DMA((5,)),
                pltpu.VMEM((width, cols), BF16),
                pltpu.VMEM((rows, cols), F32),
                pltpu.VMEM((rows, cols), F32),
                pltpu.VMEM((rows, cols), F32),
                pltpu.VMEM((rows, cols), BF16),
                pltpu.VMEM((rows, width), F32),
                pltpu.VMEM((width, rows), BF16),
                pltpu.VMEM((rows, width), F32),
                pltpu.VMEM((width, cols), F32),
                pltpu.VMEM((rows, width), BF16),
                pltpu.VMEM((rows, width), BF16),
                pltpu.VMEM((1, cols), F32),
                pltpu.VMEM((rows, width), F32),
                pltpu.VMEM((rows, 1), F32),
                pltpu.VMEM((rows, 1), F32),
                pltpu.VMEM((n_proto // 2, piece, width), F32),
                pltpu.SemaphoreType.DMA((2,)),
                pltpu.VMEM((ITERS + 1, n_patch, 1, cols), F32),
                pltpu.VMEM((ITERS + 2, n_proto, 1, rows), F32),
                pltpu.VMEM((n_proto // 2, piece, width), F32),
                pltpu.VMEM((n_proto // 2, piece, width), F32),
                pltpu.VMEM((n_patch // 2, k_piece, cols), F32),
                pltpu.VMEM((n_patch // 2, k_piece, cols), F32),
                pltpu.SemaphoreType.DMA((ITERS + 1,)),
                pltpu.SemaphoreType.DMA((ITERS + 1,)),
                pltpu.SemaphoreType.DMA((ITERS + 2,)),
                pltpu.SemaphoreType.DMA((ITERS + 2,)),
                pltpu.SemaphoreType.DMA,
                pltpu.SemaphoreType.DMA((n_proto // 2,)),
                pltpu.SemaphoreType.DMA((2,)),
                pltpu.SemaphoreType.DMA((4,)),
            ],
            compiler_params=pltpu.CompilerParams(
                collective_id=0, has_side_effects=True, vmem_limit_bytes=VLIM << 20
            ),
        )(progress_counter.reshape(1, 1), teacher_feats, student_feats, masked, prototypes)
        return tuple(
            pl.pallas_call(
                finish,
                out_shape=(
                    jax.ShapeDtypeStruct((rows,), F32),
                    jax.ShapeDtypeStruct((piece, width), F32),
                    jax.ShapeDtypeStruct((k_piece, cols), F32),
                ),
                in_specs=[vmem] * 3,
                out_specs=(vmem,) * 3,
            )(*(pltpu.with_memory_space_constraint(x, pltpu.VMEM) for x in held))
        )

    in_specs = (P("patch", None), P("patch", None), P("patch", None), P(), P(None, "proto"))
    out_specs = (P("patch"), P(("patch", "proto"), None), P("patch", "proto"))
    return jax.shard_map(shards, mesh=mesh, in_specs=in_specs, out_specs=out_specs, check_vma=False)
```

```python
import functools

import jax
import jax.numpy as jnp
from jax import lax
from jax.experimental import pallas as pl
from jax.experimental.pallas import tpu as pltpu
from jax.sharding import PartitionSpec as P

ITERS = 3
HEATUP_LENGTH = 30
LOG2E = 1.4426950408889634
MESH = pl.DeviceIdType.MESH
F32 = jnp.float32
BF16 = jnp.bfloat16
U_T, U_S, U_P, U_G = 4, 2, 8, 4
TILE, RB = 256, 256
SUBS = 4
TOTAL, CROSS = ITERS, ITERS + 1
VLIM = 62
NT = (((1,), (1,)), ((), ()))


def diagonal(size):
    return lax.broadcasted_iota(jnp.int32, (size, size), 0) == lax.broadcasted_iota(
        jnp.int32, (size, size), 1
    )


def to_row(column, eye):
    return jnp.sum(jnp.where(eye, column, 0.0), axis=0, keepdims=True)


def to_column(row, eye):
    return jnp.sum(jnp.where(eye, row, 0.0), axis=1, keepdims=True)


def remote(src, dst, send, recv, axis, peer):
    return pltpu.make_async_remote_copy(
        src_ref=src,
        dst_ref=dst,
        send_sem=send,
        recv_sem=recv,
        device_id={axis: peer},
        device_id_type=MESH,
    )


def await_bytes(ref, sem):
    pltpu.make_async_copy(ref, ref, sem).wait()


def kernel(
    n_proto,
    n_patch,
    progress_hbm,
    teacher_hbm,
    student_hbm,
    masked_hbm,
    proto_hbm,
    loss_ref,
    gs_ref,
    gp_ref,
    progress_ref,
    teacher_ref,
    student_ref,
    masked_ref,
    proto_ref,
    rw_ref,
    load_sem,
    w_hat,
    e_ref,
    s_ref,
    p_ref,
    g_ref,
    rows_ref,
    shat_t,
    ds_ref,
    dw_ref,
    t_hat,
    s_hat,
    sharp_ref,
    da_ref,
    t_ref,
    b_ref,
    feat_zero,
    feat_zero_sem,
    col_buf,
    row_buf,
    feat_one,
    feat_two,
    w_one,
    w_two,
    col_send,
    col_recv,
    row_send,
    row_recv,
    feat_one_send,
    feat_one_recv,
    feat_two_sem,
    relay_buf,
    relay_sem,
    w_one_recv,
    w_sem,
):
    me_p = lax.axis_index("proto")
    me_q = lax.axis_index("patch")
    images, slots = masked_ref.shape
    per_image = teacher_ref.shape[0] // images
    width, cols = proto_ref.shape
    rows = images * slots
    chunk = cols // 4

    loads = [
        pltpu.make_async_copy(src, dst, load_sem.at[k])
        for k, (src, dst) in enumerate(
            (
                (proto_hbm, proto_ref),
                (masked_hbm, masked_ref),
                (progress_hbm, progress_ref),
                (teacher_hbm, teacher_ref),
                (student_hbm, student_ref),
            )
        )
    ]
    for load in loads:
        load.start()

    barrier = pltpu.get_barrier_semaphore()

    def greet(axis, me, n):
        def body(d, carry):
            pl.semaphore_signal(
                barrier, inc=1, device_id={axis: lax.rem(me + d, n)}, device_id_type=MESH
            )
            return carry

        lax.fori_loop(1, n, body, 0)

    greet("proto", me_p, n_proto)
    greet("patch", me_q, n_patch)

    eye = diagonal(slots)
    lane = lax.broadcasted_iota(jnp.int32, (slots, per_image), 1)

    def block(i):
        return pl.ds(pl.multiple_of(i * slots, slots), slots)

    def gathered(ref, i):
        picks = masked_ref[pl.ds(i, 1), :]
        picks = jnp.sum(jnp.where(eye, picks, 0), axis=1, keepdims=True)
        hot = jnp.where(picks == lane, 1.0, 0.0).astype(BF16)
        at = pl.ds(pl.multiple_of(i * per_image, per_image), per_image)
        return jnp.dot(hot, ref[at, :], preferred_element_type=F32)

    def unit(x):
        return x * lax.rsqrt(jnp.sum(x * x, axis=1, keepdims=True) + 1e-12)

    def folded(x):
        return jnp.sum(x.reshape(slots // 8, 8, cols), axis=0)

    loads[0].wait()
    w_raw = proto_ref[...].astype(F32)
    r_w = lax.rsqrt(jnp.sum(w_raw * w_raw, axis=0, keepdims=True) + 1e-12)
    rw_ref[...] = r_w
    w_hat[...] = (w_raw * r_w).astype(BF16)

    loads[2].wait()
    steps = jnp.broadcast_to(progress_ref[...].astype(F32), (1, cols))
    sharp_ref[...] = LOG2E / (0.04 + 0.03 * steps / HEATUP_LENGTH)

    def teacher_rows(i, carry):
        t_hat[block(i), :] = unit(gathered(teacher_ref, i)).astype(BF16)
        return carry

    def teacher_tile(j, carry):
        at = pl.ds(pl.multiple_of(j * TILE, TILE), TILE)
        total = None
        for k in range(rows // RB):
            here = pl.ds(k * RB, RB)
            e = jnp.dot(t_hat[here, :], w_hat[:, at], preferred_element_type=F32)
            e = jnp.exp2(e * sharp_ref[:, at])
            e_ref[here, at] = e
            part_sum = jnp.sum(e.reshape(RB // 8, 8, TILE), axis=0)
            total = part_sum if total is None else total + part_sum
        col_buf[0, me_q, :, at] = jnp.sum(total, axis=0, keepdims=True)
        return carry

    def student_rows(i, carry):
        x = gathered(student_ref, i)
        rows_ref[block(i), :] = x
        s_unit = unit(x)
        s_hat[block(i), :] = s_unit.astype(BF16)
        shat_t[:, block(i)] = s_unit.T.astype(BF16)
        return carry

    def student_block(i, carry):
        s = jnp.dot(s_hat[block(i), :], w_hat[...], preferred_element_type=F32)
        s_ref[block(i), :] = s
        p = jnp.exp2(s * (10.0 * LOG2E))
        p_ref[block(i), :] = p
        total = jnp.sum(p, axis=1, keepdims=True)
        row_buf[TOTAL, me_p, :, block(i)] = to_row(total, eye)
        return carry

    def spread(x):
        high = x.astype(BF16)
        low = (x - high.astype(F32)).astype(BF16)
        w = w_hat[...]
        return lax.dot_general(high, w, NT, preferred_element_type=F32) + lax.dot_general(
            low, w, NT, preferred_element_type=F32
        )

    def a_block(i, carry):
        da_ref[block(i), :] = spread(p_ref[block(i), :])
        return carry

    def b_block(i, carry):
        ds_ref[block(i), :] = spread(e_ref[block(i), :])
        return carry

    def send_all(buf, axis, me, n, send, recv):
        def body(k, carry):
            peer = jnp.bitwise_xor(me, n - 1 - k)
            remote(buf.at[me], buf.at[me], send, recv, axis, peer).start()
            return carry

        lax.fori_loop(0, n - 1, body, 0, unroll=n <= 8)

    def wait_all(buf, n, send, recv):
        await_bytes(buf.at[pl.ds(0, n - 1)], recv)
        await_bytes(buf.at[pl.ds(0, n - 1)], send)

    def column_pass(b_row_at, acc0):
        def body(i, acc):
            b_col = to_column(b_row_at(i), eye)
            return acc + folded(e_ref[block(i), :] * b_col)

        return lax.fori_loop(0, images, body, acc0, unroll=U_P)

    half = n_proto // 2
    hi, lo = me_p // 2, lax.rem(me_p, 2)
    other = 1 - lo
    piece = rows // n_proto
    whole_blocks = n_proto == images
    subs = feat_one_recv.shape[1]
    sub = piece // subs
    relays = False
    upper = (2 * hi) // half

    def far_first(j):
        down = half - 1 - j - (j + hi + 1) // half
        up = j + (j + half - hi) // half
        return (1 - upper) * down + upper * up

    def place(j):
        return far_first(j) if j < half - 1 else hi

    def part(ref, o, size):
        return ref.at[pl.ds(pl.multiple_of(o * size, size), size), :]

    def a_pair(o_hi):
        remote(
            part(da_ref, o_hi * 2 + other, piece),
            feat_zero.at[o_hi],
            feat_zero_sem.at[0],
            feat_zero_sem.at[1],
            "proto",
            hi * 2 + other,
        ).start()

    def sub_part(ref, o, k):
        return ref.at[pl.ds(pl.multiple_of(o * piece + k * sub, sub), sub), :]

    def sub_slot(ref, o_hi, k):
        return ref.at[o_hi, pl.ds(k * sub, sub), :]

    def b_pair(o_hi):
        for k in range(subs):
            remote(
                sub_part(ds_ref, o_hi * 2 + other, k),
                sub_slot(feat_one, o_hi, k),
                feat_one_send,
                feat_one_recv.at[o_hi, k],
                "proto",
                hi * 2 + other,
            ).start()

    def each(n, f):
        def body(j, carry):
            f(j)
            return carry

        lax.fori_loop(0, n, body, 0)

    zero = jnp.zeros((8, cols), F32)
    loads[1].wait()
    loads[3].wait()
    lax.fori_loop(0, images, teacher_rows, 0, unroll=True)
    lax.fori_loop(0, cols // TILE, teacher_tile, 0, unroll=U_T)
    loads[4].wait()
    pl.semaphore_wait(barrier, n_proto + n_patch - 2)

    def send_rows(k):
        send_all(row_buf.at[k], "proto", me_p, n_proto, row_send.at[k], row_recv.at[k])

    def wait_rows(k):
        wait_all(row_buf.at[k], n_proto, row_send.at[k], row_recv.at[k])

    def send_cols(k):
        send_all(col_buf.at[k], "patch", me_q, n_patch, col_send.at[k], col_recv.at[k])

    def wait_cols(k):
        wait_all(col_buf.at[k], n_patch, col_send.at[k], col_recv.at[k])

    def row_pass(it):
        a_row = 1.0 / jnp.sum(col_buf[it], axis=0)

        def body(i, carry):
            ea = e_ref[block(i), :] * a_row
            if it + 1 == ITERS:
                e_ref[block(i), :] = ea
            row_buf[it, me_p, :, block(i)] = to_row(jnp.sum(ea, axis=1, keepdims=True), eye)
            return carry

        lax.fori_loop(0, images, body, 0, unroll=U_P)
        send_rows(it)

    def col_pass(it):
        loss_ref[...] = 1.0 / jnp.sum(row_buf[it], axis=0)
        acc = column_pass(lambda i: loss_ref[:, block(i)], zero)
        col_buf[it + 1, me_q, :, :] = jnp.sum(acc, axis=0, keepdims=True)
        send_cols(it + 1)

    send_cols(0)
    lax.fori_loop(0, images, student_rows, 0, unroll=U_S)
    if whole_blocks:
        student_block(2 * place(0) + other, 0)
    wait_cols(0)

    row_pass(0)
    if whole_blocks:
        a_block(2 * place(0) + other, 0)
        a_pair(place(0))
        student_block(2 * place(1) + other, 0)
        a_block(2 * place(1) + other, 0)
        a_pair(place(1))
        for j in range(2, half):
            student_block(2 * place(j) + other, 0)
        student_block(lo, 0)
    else:
        lax.fori_loop(0, images, student_block, 0, unroll=U_S)
    wait_rows(0)
    col_pass(0)
    if whole_blocks:
        for j in range(1, half):
            student_block(2 * j + lo, 0)
    wait_cols(1)

    row_pass(1)
    send_rows(TOTAL)
    if whole_blocks:
        for j in range(2, half):
            a_block(2 * place(j) + other, 0)
            a_pair(place(j))
        for j in range(half):
            a_block(2 * j + lo, 0)
    else:
        lax.fori_loop(0, images, a_block, 0, unroll=U_S)
        each(half, a_pair)
    wait_rows(1)
    col_pass(1)

    wait_rows(TOTAL)
    totals = jnp.sum(row_buf[TOTAL], axis=0)
    scale = 1.0 / (0.1 * rows * n_patch)
    col_buf[0, 1, :, :] = scale / totals

    def weigh(i, carry):
        t_col = to_column(col_buf[0, 1, :, block(i)], eye)
        t_ref[block(i), :] = t_col
        p_ref[block(i), :] = p_ref[block(i), :] * t_col
        return carry

    lax.fori_loop(0, images, weigh, 0, unroll=U_S)
    wait_cols(2)

    row_pass(2)

    def cross_body(i, carry):
        x = jnp.sum(e_ref[block(i), :] * s_ref[block(i), :], axis=1, keepdims=True)
        row_buf[CROSS, me_p, :, block(i)] = to_row(x, eye)
        return carry

    def cross():
        lax.fori_loop(0, images, cross_body, 0, unroll=U_S)
        send_rows(CROSS)

    if whole_blocks:
        for j in range(half):
            b_block(2 * place(j) + other, 0)
            b_pair(place(j))
            if j == 0:
                cross()
        for j in range(half):
            b_block(2 * j + lo, 0)
    else:
        lax.fori_loop(0, images, b_block, 0, unroll=U_S)
        cross()
        each(half, b_pair)

    await_bytes(feat_zero, feat_zero_sem.at[1])

    def join(g):
        mine = part(da_ref, 2 * g + lo, piece)
        mine[...] = (mine[...] + feat_zero[g]) * part(t_ref, 2 * g + lo, piece)[...]

    each(half, join)
    wait_rows(2)
    b_row = 1.0 / jnp.sum(row_buf[2], axis=0)
    col_buf[0, 0, :, :] = b_row * scale

    def to_b(i, carry):
        b_ref[block(i), :] = to_column(col_buf[0, 0, :, block(i)], eye)
        return carry

    lax.fori_loop(0, images, to_b, 0, unroll=U_P)

    def feat_add(o_hi, k):
        await_bytes(sub_slot(feat_one, o_hi, k), feat_one_recv.at[o_hi, k])
        o = o_hi * 2 + lo
        both = sub_part(ds_ref, o, k)[...] + feat_one[o_hi, pl.ds(k * sub, sub), :]
        return sub_part(da_ref, o, k)[...] - sub_part(b_ref, o, k)[...] * both

    def feat_send(o_hi, k):
        remote(
            sub_part(da_ref, o_hi * 2 + lo, k),
            sub_slot(feat_two, hi, k),
            feat_two_sem.at[0],
            feat_two_sem.at[1],
            "proto",
            o_hi * 2 + lo,
        ).start()

    def direct(j, k):
        o_hi = far_first(j)
        sub_part(da_ref, o_hi * 2 + lo, k)[...] = feat_add(o_hi, k)
        feat_send(o_hi, k)

    outer = jnp.logical_or(hi == 0, hi == half - 1)
    inner = jnp.logical_not(outer)
    nearer = 1 - upper + 2 * upper

    def second(k):
        o_hi = far_first(1)
        mine = sub_part(da_ref, o_hi * 2 + lo, k)
        mine[...] = feat_add(o_hi, k)

        @pl.when(outer)
        def _():
            remote(
                mine,
                relay_buf.at[pl.ds(k * sub, sub), :],
                feat_two_sem.at[0],
                relay_sem.at[k],
                "proto",
                nearer * 2 + lo,
            ).start()

    def relayed(k):
        @pl.when(inner)
        def _():
            o_hi = far_first(1)
            got = relay_buf.at[pl.ds(k * sub, sub), :]
            await_bytes(got, relay_sem.at[k])
            mine = sub_part(da_ref, o_hi * 2 + lo, k)
            mine[...] = mine[...] + got[...]
            feat_send(o_hi, k)

    k_piece = width // n_patch
    q_half = n_patch // 2
    q_hi, q_lo = me_q // 2, lax.rem(me_q, 2)
    q_other = 1 - q_lo

    def w_slab(ref, o, j):
        return ref.at[
            pl.ds(pl.multiple_of(o * k_piece, k_piece), k_piece), pl.ds(j * chunk, chunk)
        ]

    def dw_chunk(j):
        at = pl.ds(j * chunk, chunk)
        g = (p_ref[:, at] - e_ref[:, at] * b_ref[...]).astype(BF16)
        dw = jnp.dot(shat_t[...], g, preferred_element_type=F32)
        dw_ref[:, at] = dw

        def w_pair(d, carry):
            o_hi = lax.rem(q_hi + d, q_half)
            remote(
                w_slab(dw_ref, o_hi * 2 + q_other, j),
                w_one.at[o_hi, :, at],
                w_sem.at[0],
                w_one_recv.at[j],
                "patch",
                q_hi * 2 + q_other,
            ).start()
            return carry

        lax.fori_loop(1, q_half + 1, w_pair, 0)
        col_buf[ITERS, me_q, :, at] = jnp.sum(
            dw * proto_ref[:, at].astype(F32), axis=0, keepdims=True
        )

    def w_rest(j):
        at = pl.ds(j * chunk, chunk)
        await_bytes(w_one.at[:, :, at], w_one_recv.at[j])

        def body(d, carry):
            o_hi = lax.rem(q_hi + d, q_half)
            mine = w_slab(dw_ref, o_hi * 2 + q_lo, j)
            mine[...] = mine[...] + w_one[o_hi, :, at]
            remote(
                mine,
                w_two.at[q_hi, :, at],
                w_sem.at[2],
                w_sem.at[3],
                "patch",
                o_hi * 2 + q_lo,
            ).start()
            return carry

        lax.fori_loop(1, q_half, body, 0)

    if whole_blocks:
        for k in range(subs // 2):
            direct(0, k)
    for j in range(cols // chunk):
        dw_chunk(j)
    dots = col_buf.at[ITERS]
    send_cols(ITERS)
    if whole_blocks:
        for k in range(subs // 2, subs):
            direct(0, k)
    for j in range(cols // chunk):
        w_rest(j)
    if whole_blocks and relays:
        for k in range(subs):
            second(k)
        for k in range(subs):
            direct(2, k)
            relayed(k)
    else:

        def all_direct(j, carry):
            for k in range(subs):
                direct(j, k)
            return carry

        lax.fori_loop(1 if whole_blocks else 0, half - 1, all_direct, 0)
    w_two[q_hi, :, :] = part(dw_ref, me_q, k_piece)[...] + w_one[q_hi]
    for k in range(subs):
        feat_two[hi, pl.ds(k * sub, sub), :] = feat_add(hi, k)

    wait_all(dots, n_patch, col_send.at[ITERS], col_recv.at[ITERS])
    await_bytes(w_two.at[pl.ds(0, q_half - 1)], w_sem.at[3])
    wait_rows(CROSS)
    loss_ref[...] = jnp.log(totals) - 10.0 * jnp.sum(row_buf[CROSS], axis=0) * b_row
    dot = jnp.sum(col_buf[ITERS], axis=0)
    r_w = rw_ref[...]
    w_mine = part(proto_ref, me_q, k_piece)[...].astype(F32)
    gp_ref[...] = r_w * jnp.sum(w_two[...], axis=0) - w_mine * (r_w * r_w * r_w * dot)

    if whole_blocks and relays:

        @pl.when(outer)
        def _():
            await_bytes(feat_two.at[pl.ds(0, half - 1)], feat_two_sem.at[1])

        @pl.when(inner)
        def _():
            feat_two[lax.rem(hi + 2, half), :, :] = jnp.zeros((piece, width), F32)
            await_bytes(feat_two.at[pl.ds(0, half - 2)], feat_two_sem.at[1])

    else:
        await_bytes(feat_two.at[pl.ds(0, half - 1)], feat_two_sem.at[1])
    x = part(rows_ref, me_p, piece)[...]
    g = jnp.sum(feat_two[...], axis=0)
    r = lax.rsqrt(jnp.sum(x * x, axis=1, keepdims=True) + 1e-12)
    gs_ref[...] = r * g - x * (r * r * r * jnp.sum(x * g, axis=1, keepdims=True))

    await_bytes(w_one, w_sem.at[0])
    await_bytes(w_two.at[pl.ds(0, q_half - 1)], w_sem.at[2])
    await_bytes(feat_zero, feat_zero_sem.at[0])
    await_bytes(feat_one, feat_one_send)
    await_bytes(feat_two.at[pl.ds(0, half - 1)], feat_two_sem.at[0])


def finish(loss_in, gs_in, gp_in, loss_ref, gs_ref, gp_ref):
    loss_ref[...] = loss_in[...].reshape(loss_ref.shape)
    gs_ref[...] = gs_in[...]
    gp_ref[...] = gp_in[...]


def solution(mesh):
    n_proto, n_patch = mesh.shape["proto"], mesh.shape["patch"]

    def shards(teacher_feats, student_feats, masked, progress_counter, prototypes):
        images, slots = masked.shape
        rows = images * slots
        width, cols = prototypes.shape
        piece, k_piece = rows // n_proto, width // n_patch
        subs = SUBS if piece % (8 * SUBS) == 0 else 1
        vmem = pl.BlockSpec(memory_space=pltpu.VMEM)
        held = pl.pallas_call(
            functools.partial(kernel, n_proto, n_patch),
            out_shape=(
                pltpu.VMEM((1, rows), F32),
                pltpu.VMEM((piece, width), F32),
                pltpu.VMEM((k_piece, cols), F32),
            ),
            in_specs=[pl.BlockSpec(memory_space=pltpu.HBM)] * 5,
            out_specs=(vmem, vmem, vmem),
            scratch_shapes=[
                pltpu.VMEM((1, 1), jnp.int32),
                pltpu.VMEM(teacher_feats.shape, BF16),
                pltpu.VMEM(student_feats.shape, BF16),
                pltpu.VMEM(masked.shape, jnp.int32),
                pltpu.VMEM(prototypes.shape, BF16),
                pltpu.VMEM((1, cols), F32),
                pltpu.SemaphoreType.DMA((5,)),
                pltpu.VMEM((width, cols), BF16),
                pltpu.VMEM((rows, cols), F32),
                pltpu.VMEM((rows, cols), F32),
                pltpu.VMEM((rows, cols), F32),
                pltpu.VMEM((rows, cols), BF16),
                pltpu.VMEM((rows, width), F32),
                pltpu.VMEM((width, rows), BF16),
                pltpu.VMEM((rows, width), F32),
                pltpu.VMEM((width, cols), F32),
                pltpu.VMEM((rows, width), BF16),
                pltpu.VMEM((rows, width), BF16),
                pltpu.VMEM((1, cols), F32),
                pltpu.VMEM((rows, width), F32),
                pltpu.VMEM((rows, 1), F32),
                pltpu.VMEM((rows, 1), F32),
                pltpu.VMEM((n_proto // 2, piece, width), F32),
                pltpu.SemaphoreType.DMA((2,)),
                pltpu.VMEM((ITERS + 1, n_patch, 1, cols), F32),
                pltpu.VMEM((ITERS + 2, n_proto, 1, rows), F32),
                pltpu.VMEM((n_proto // 2, piece, width), F32),
                pltpu.VMEM((n_proto // 2, piece, width), F32),
                pltpu.VMEM((n_patch // 2, k_piece, cols), F32),
                pltpu.VMEM((n_patch // 2, k_piece, cols), F32),
                pltpu.SemaphoreType.DMA((ITERS + 1,)),
                pltpu.SemaphoreType.DMA((ITERS + 1,)),
                pltpu.SemaphoreType.DMA((ITERS + 2,)),
                pltpu.SemaphoreType.DMA((ITERS + 2,)),
                pltpu.SemaphoreType.DMA,
                pltpu.SemaphoreType.DMA((n_proto // 2, subs)),
                pltpu.SemaphoreType.DMA((2,)),
                pltpu.VMEM((piece, width), F32),
                pltpu.SemaphoreType.DMA((subs,)),
                pltpu.SemaphoreType.DMA((4,)),
                pltpu.SemaphoreType.DMA((4,)),
            ],
            compiler_params=pltpu.CompilerParams(
                collective_id=0, has_side_effects=True, vmem_limit_bytes=VLIM << 20
            ),
        )(progress_counter.reshape(1, 1), teacher_feats, student_feats, masked, prototypes)
        return tuple(
            pl.pallas_call(
                finish,
                out_shape=(
                    jax.ShapeDtypeStruct((rows,), F32),
                    jax.ShapeDtypeStruct((piece, width), F32),
                    jax.ShapeDtypeStruct((k_piece, cols), F32),
                ),
                in_specs=[vmem] * 3,
                out_specs=(vmem,) * 3,
            )(*(pltpu.with_memory_space_constraint(x, pltpu.VMEM) for x in held))
        )

    in_specs = (P("patch", None), P("patch", None), P("patch", None), P(), P(None, "proto"))
    out_specs = (P("patch"), P(("patch", "proto"), None), P("patch", "proto"))
    return jax.shard_map(shards, mesh=mesh, in_specs=in_specs, out_specs=out_specs, check_vma=False)
```

```python
import functools

import jax
import jax.numpy as jnp
from jax import lax
from jax.experimental import pallas as pl
from jax.experimental.pallas import tpu as pltpu
from jax.sharding import PartitionSpec as P

ITERS = 3
HEATUP_LENGTH = 30
LOG2E = 1.4426950408889634
MESH = pl.DeviceIdType.MESH
F32 = jnp.float32
BF16 = jnp.bfloat16
U_T, U_S, U_P, U_G = 4, 2, 8, 4
TILE, RB = 256, 256
SUBS = 4
TOTAL, CROSS = ITERS, ITERS + 1
VLIM = 62
NT = (((1,), (1,)), ((), ()))


def diagonal(size):
    return lax.broadcasted_iota(jnp.int32, (size, size), 0) == lax.broadcasted_iota(
        jnp.int32, (size, size), 1
    )


def to_row(column, eye):
    return jnp.sum(jnp.where(eye, column, 0.0), axis=0, keepdims=True)


def to_column(row, eye):
    return jnp.sum(jnp.where(eye, row, 0.0), axis=1, keepdims=True)


def remote(src, dst, send, recv, axis, peer):
    return pltpu.make_async_remote_copy(
        src_ref=src,
        dst_ref=dst,
        send_sem=send,
        recv_sem=recv,
        device_id={axis: peer},
        device_id_type=MESH,
    )


def await_bytes(ref, sem):
    pltpu.make_async_copy(ref, ref, sem).wait()


def kernel(
    n_proto,
    n_patch,
    progress_hbm,
    teacher_hbm,
    student_hbm,
    masked_hbm,
    proto_hbm,
    loss_ref,
    gs_ref,
    gp_ref,
    progress_ref,
    teacher_ref,
    student_ref,
    masked_ref,
    proto_ref,
    rw_ref,
    load_sem,
    w_hat,
    e_ref,
    s_ref,
    p_ref,
    g_ref,
    rows_ref,
    shat_t,
    ds_ref,
    dw_ref,
    t_hat,
    s_hat,
    sharp_ref,
    da_ref,
    t_ref,
    b_ref,
    feat_zero,
    feat_zero_sem,
    col_buf,
    row_buf,
    feat_one,
    feat_two,
    w_one,
    w_two,
    col_send,
    col_recv,
    row_send,
    row_recv,
    feat_one_send,
    feat_one_recv,
    feat_two_sem,
    early_buf,
    early_sem,
    w_one_recv,
    w_sem,
):
    me_p = lax.axis_index("proto")
    me_q = lax.axis_index("patch")
    images, slots = masked_ref.shape
    per_image = teacher_ref.shape[0] // images
    width, cols = proto_ref.shape
    rows = images * slots
    chunk = cols // 4

    loads = [
        pltpu.make_async_copy(src, dst, load_sem.at[k])
        for k, (src, dst) in enumerate(
            (
                (proto_hbm, proto_ref),
                (masked_hbm, masked_ref),
                (progress_hbm, progress_ref),
                (teacher_hbm, teacher_ref),
                (student_hbm, student_ref),
            )
        )
    ]
    for load in loads:
        load.start()

    barrier = pltpu.get_barrier_semaphore()

    def greet(axis, me, n):
        def body(d, carry):
            pl.semaphore_signal(
                barrier, inc=1, device_id={axis: lax.rem(me + d, n)}, device_id_type=MESH
            )
            return carry

        lax.fori_loop(1, n, body, 0)

    greet("proto", me_p, n_proto)
    greet("patch", me_q, n_patch)

    eye = diagonal(slots)
    lane = lax.broadcasted_iota(jnp.int32, (slots, per_image), 1)

    def block(i):
        return pl.ds(pl.multiple_of(i * slots, slots), slots)

    def gathered(ref, i):
        picks = masked_ref[pl.ds(i, 1), :]
        picks = jnp.sum(jnp.where(eye, picks, 0), axis=1, keepdims=True)
        hot = jnp.where(picks == lane, 1.0, 0.0).astype(BF16)
        at = pl.ds(pl.multiple_of(i * per_image, per_image), per_image)
        return jnp.dot(hot, ref[at, :], preferred_element_type=F32)

    def unit(x):
        return x * lax.rsqrt(jnp.sum(x * x, axis=1, keepdims=True) + 1e-12)

    def folded(x):
        return jnp.sum(x.reshape(slots // 8, 8, cols), axis=0)

    loads[0].wait()
    w_raw = proto_ref[...].astype(F32)
    r_w = lax.rsqrt(jnp.sum(w_raw * w_raw, axis=0, keepdims=True) + 1e-12)
    rw_ref[...] = r_w
    w_hat[...] = (w_raw * r_w).astype(BF16)

    loads[2].wait()
    steps = jnp.broadcast_to(progress_ref[...].astype(F32), (1, cols))
    sharp_ref[...] = LOG2E / (0.04 + 0.03 * steps / HEATUP_LENGTH)

    def teacher_rows(i, carry):
        t_hat[block(i), :] = unit(gathered(teacher_ref, i)).astype(BF16)
        return carry

    def teacher_tile(j, carry):
        at = pl.ds(pl.multiple_of(j * TILE, TILE), TILE)
        total = None
        for k in range(rows // RB):
            here = pl.ds(k * RB, RB)
            e = jnp.dot(t_hat[here, :], w_hat[:, at], preferred_element_type=F32)
            e = jnp.exp2(e * sharp_ref[:, at])
            e_ref[here, at] = e
            part_sum = jnp.sum(e.reshape(RB // 8, 8, TILE), axis=0)
            total = part_sum if total is None else total + part_sum
        col_buf[0, me_q, :, at] = jnp.sum(total, axis=0, keepdims=True)
        return carry

    def student_rows(i, carry):
        x = gathered(student_ref, i)
        rows_ref[block(i), :] = x
        s_unit = unit(x)
        s_hat[block(i), :] = s_unit.astype(BF16)
        shat_t[:, block(i)] = s_unit.T.astype(BF16)
        return carry

    def student_block(i, carry):
        s = jnp.dot(s_hat[block(i), :], w_hat[...], preferred_element_type=F32)
        s_ref[block(i), :] = s
        p = jnp.exp2(s * (10.0 * LOG2E))
        p_ref[block(i), :] = p
        total = jnp.sum(p, axis=1, keepdims=True)
        row_buf[TOTAL, me_p, :, block(i)] = to_row(total, eye)
        return carry

    def spread(x):
        high = x.astype(BF16)
        low = (x - high.astype(F32)).astype(BF16)
        both = jnp.concatenate([high, low], axis=0)
        out = lax.dot_general(both, w_hat[...], NT, preferred_element_type=F32)
        return out[:slots] + out[slots:]

    def a_block(i, carry):
        da_ref[block(i), :] = spread(p_ref[block(i), :])
        return carry

    def b_block(i, carry):
        ds_ref[block(i), :] = spread(e_ref[block(i), :])
        return carry

    def send_all(buf, axis, me, n, send, recv):
        def body(k, carry):
            peer = jnp.bitwise_xor(me, n - 1 - k)
            remote(buf.at[me], buf.at[me], send, recv, axis, peer).start()
            return carry

        lax.fori_loop(0, n - 1, body, 0, unroll=n <= 8)

    def wait_all(buf, n, send, recv):
        await_bytes(buf.at[pl.ds(0, n - 1)], recv)
        await_bytes(buf.at[pl.ds(0, n - 1)], send)

    def column_pass(b_row_at, acc0):
        def body(i, acc):
            b_col = to_column(b_row_at(i), eye)
            return acc + folded(e_ref[block(i), :] * b_col)

        return lax.fori_loop(0, images, body, acc0, unroll=U_P)

    half = n_proto // 2
    hi, lo = me_p // 2, lax.rem(me_p, 2)
    other = 1 - lo
    piece = rows // n_proto
    whole_blocks = n_proto == images
    subs = feat_one_recv.shape[1]
    sub = piece // subs
    ahead = subs // 2 if whole_blocks and half == 4 else 0
    head = ahead * sub
    upper = (2 * hi) // half

    def far_first(j):
        down = half - 1 - j - (j + hi + 1) // half
        up = j + (j + half - hi) // half
        return (1 - upper) * down + upper * up

    def place(j):
        return far_first(j) if j < half - 1 else hi

    def part(ref, o, size):
        return ref.at[pl.ds(pl.multiple_of(o * size, size), size), :]

    def a_pair(o_hi, at=1):
        remote(
            part(da_ref, o_hi * 2 + other, piece),
            feat_zero.at[o_hi],
            feat_zero_sem.at[0],
            feat_zero_sem.at[at],
            "proto",
            hi * 2 + other,
        ).start()

    def sub_part(ref, o, k):
        return ref.at[pl.ds(pl.multiple_of(o * piece + k * sub, sub), sub), :]

    def sub_slot(ref, o_hi, k):
        return ref.at[o_hi, pl.ds(k * sub, sub), :]

    def b_pair(o_hi):
        for k in range(subs):
            remote(
                sub_part(ds_ref, o_hi * 2 + other, k),
                sub_slot(feat_one, o_hi, k),
                feat_one_send,
                feat_one_recv.at[o_hi, k],
                "proto",
                hi * 2 + other,
            ).start()

    def early(ref, got, out, k):
        o_hi = place(0)
        mine = sub_part(ref, o_hi * 2 + lo, k)
        mine[...] = mine[...] + got[o_hi, pl.ds(k * sub, sub), :]
        remote(
            mine,
            early_buf.at[out, lax.rem(hi, 2), pl.ds(k * sub, sub), :],
            early_sem.at[out, 0],
            early_sem.at[out, 1],
            "proto",
            o_hi * 2 + lo,
        ).start()

    def each(n, f):
        def body(j, carry):
            f(j)
            return carry

        lax.fori_loop(0, n, body, 0)

    zero = jnp.zeros((8, cols), F32)
    loads[1].wait()
    loads[3].wait()
    lax.fori_loop(0, images, teacher_rows, 0, unroll=True)
    lax.fori_loop(0, cols // TILE, teacher_tile, 0, unroll=U_T)
    loads[4].wait()
    pl.semaphore_wait(barrier, n_proto + n_patch - 2)

    def send_rows(k):
        send_all(row_buf.at[k], "proto", me_p, n_proto, row_send.at[k], row_recv.at[k])

    def wait_rows(k):
        wait_all(row_buf.at[k], n_proto, row_send.at[k], row_recv.at[k])

    def send_cols(k):
        send_all(col_buf.at[k], "patch", me_q, n_patch, col_send.at[k], col_recv.at[k])

    def wait_cols(k):
        wait_all(col_buf.at[k], n_patch, col_send.at[k], col_recv.at[k])

    def row_pass(it):
        a_row = 1.0 / jnp.sum(col_buf[it], axis=0)

        def body(i, carry):
            ea = e_ref[block(i), :] * a_row
            if it + 1 == ITERS:
                e_ref[block(i), :] = ea
            row_buf[it, me_p, :, block(i)] = to_row(jnp.sum(ea, axis=1, keepdims=True), eye)
            return carry

        lax.fori_loop(0, images, body, 0, unroll=U_P)
        send_rows(it)

    def col_pass(it):
        loss_ref[...] = 1.0 / jnp.sum(row_buf[it], axis=0)
        acc = column_pass(lambda i: loss_ref[:, block(i)], zero)
        col_buf[it + 1, me_q, :, :] = jnp.sum(acc, axis=0, keepdims=True)
        send_cols(it + 1)

    send_cols(0)
    lax.fori_loop(0, images, student_rows, 0, unroll=U_S)
    if whole_blocks:
        student_block(2 * place(0) + other, 0)
    wait_cols(0)

    row_pass(0)
    if whole_blocks:
        a_block(2 * place(0) + other, 0)
        a_pair(place(0), 2 if ahead else 1)
        student_block(2 * place(1) + other, 0)
        a_block(2 * place(1) + other, 0)
        a_pair(place(1))
        for j in range(2, half):
            student_block(2 * place(j) + other, 0)
        student_block(lo, 0)
    else:
        lax.fori_loop(0, images, student_block, 0, unroll=U_S)
    wait_rows(0)
    col_pass(0)
    if whole_blocks:
        for j in range(1, half):
            student_block(2 * j + lo, 0)
    wait_cols(1)

    row_pass(1)
    send_rows(TOTAL)
    if whole_blocks:
        for j in range(2, half):
            a_block(2 * place(j) + other, 0)
            a_pair(place(j))
        for j in range(half):
            a_block(2 * j + lo, 0)
    else:
        lax.fori_loop(0, images, a_block, 0, unroll=U_S)
        each(half, a_pair)
    wait_rows(1)
    col_pass(1)

    if ahead:
        await_bytes(feat_zero.at[place(0)], feat_zero_sem.at[2])
        for k in range(ahead):
            early(da_ref, feat_zero, 0, k)
    wait_rows(TOTAL)
    totals = jnp.sum(row_buf[TOTAL], axis=0)
    scale = 1.0 / (0.1 * rows * n_patch)
    col_buf[0, 1, :, :] = scale / totals

    def weigh(i, carry):
        t_col = to_column(col_buf[0, 1, :, block(i)], eye)
        t_ref[block(i), :] = t_col
        p_ref[block(i), :] = p_ref[block(i), :] * t_col
        return carry

    lax.fori_loop(0, images, weigh, 0, unroll=U_S)
    wait_cols(2)

    row_pass(2)

    def cross_body(i, carry):
        x = jnp.sum(e_ref[block(i), :] * s_ref[block(i), :], axis=1, keepdims=True)
        row_buf[CROSS, me_p, :, block(i)] = to_row(x, eye)
        return carry

    def cross():
        lax.fori_loop(0, images, cross_body, 0, unroll=U_S)
        send_rows(CROSS)

    if whole_blocks:
        for j in range(half):
            b_block(2 * place(j) + other, 0)
            b_pair(place(j))
            if j == 0:
                cross()
        for j in range(half):
            b_block(2 * place(j) + lo, 0)
    else:
        lax.fori_loop(0, images, b_block, 0, unroll=U_S)
        cross()
        each(half, b_pair)

    def join(g):
        mine = part(da_ref, 2 * g + lo, piece)
        mine[...] = (mine[...] + feat_zero[g]) * part(t_ref, 2 * g + lo, piece)[...]

    if ahead:
        await_bytes(feat_zero.at[pl.ds(0, half - 1)], feat_zero_sem.at[1])
        for k in range(ahead, subs):
            mine = sub_part(da_ref, 2 * place(0) + lo, k)
            got = feat_zero[place(0), pl.ds(k * sub, sub), :]
            mine[...] = (mine[...] + got) * sub_part(t_ref, 2 * place(0) + lo, k)[...]
        for j in range(1, half):
            join(place(j))
        for k in range(ahead):
            await_bytes(sub_slot(feat_one, place(0), k), feat_one_recv.at[place(0), k])
            early(ds_ref, feat_one, 1, k)
    else:
        await_bytes(feat_zero, feat_zero_sem.at[1])
        each(half, join)
    wait_rows(2)
    b_row = 1.0 / jnp.sum(row_buf[2], axis=0)
    col_buf[0, 0, :, :] = b_row * scale

    def to_b(i, carry):
        b_ref[block(i), :] = to_column(col_buf[0, 0, :, block(i)], eye)
        return carry

    lax.fori_loop(0, images, to_b, 0, unroll=U_P)

    def feat_add(o_hi, k):
        await_bytes(sub_slot(feat_one, o_hi, k), feat_one_recv.at[o_hi, k])
        o = o_hi * 2 + lo
        both = sub_part(ds_ref, o, k)[...] + feat_one[o_hi, pl.ds(k * sub, sub), :]
        return sub_part(da_ref, o, k)[...] - sub_part(b_ref, o, k)[...] * both

    def feat_send(o_hi, k):
        remote(
            sub_part(da_ref, o_hi * 2 + lo, k),
            sub_slot(feat_two, hi, k),
            feat_two_sem.at[0],
            feat_two_sem.at[1],
            "proto",
            o_hi * 2 + lo,
        ).start()

    def direct(j, k):
        o_hi = far_first(j)
        sub_part(da_ref, o_hi * 2 + lo, k)[...] = feat_add(o_hi, k)
        feat_send(o_hi, k)

    k_piece = width // n_patch
    q_half = n_patch // 2
    q_hi, q_lo = me_q // 2, lax.rem(me_q, 2)
    q_other = 1 - q_lo

    def w_slab(ref, o, j):
        return ref.at[
            pl.ds(pl.multiple_of(o * k_piece, k_piece), k_piece), pl.ds(j * chunk, chunk)
        ]

    def dw_chunk(j):
        at = pl.ds(j * chunk, chunk)
        g = (p_ref[:, at] - e_ref[:, at] * b_ref[...]).astype(BF16)
        dw = jnp.dot(shat_t[...], g, preferred_element_type=F32)
        dw_ref[:, at] = dw

        def w_pair(d, carry):
            o_hi = lax.rem(q_hi + d, q_half)
            remote(
                w_slab(dw_ref, o_hi * 2 + q_other, j),
                w_one.at[o_hi, :, at],
                w_sem.at[0],
                w_one_recv.at[j],
                "patch",
                q_hi * 2 + q_other,
            ).start()
            return carry

        lax.fori_loop(1, q_half + 1, w_pair, 0)
        col_buf[ITERS, me_q, :, at] = jnp.sum(
            dw * proto_ref[:, at].astype(F32), axis=0, keepdims=True
        )

    def w_rest(j):
        at = pl.ds(j * chunk, chunk)
        await_bytes(w_one.at[:, :, at], w_one_recv.at[j])

        def body(d, carry):
            o_hi = lax.rem(q_hi + d, q_half)
            mine = w_slab(dw_ref, o_hi * 2 + q_lo, j)
            mine[...] = mine[...] + w_one[o_hi, :, at]
            remote(
                mine,
                w_two.at[q_hi, :, at],
                w_sem.at[2],
                w_sem.at[3],
                "patch",
                o_hi * 2 + q_lo,
            ).start()
            return carry

        lax.fori_loop(1, q_half, body, 0)

    if whole_blocks:
        for k in range(ahead, ahead + (subs - ahead) // 2):
            direct(0, k)
    for j in range(cols // chunk):
        dw_chunk(j)
    dots = col_buf.at[ITERS]
    send_cols(ITERS)
    if whole_blocks:
        for k in range(ahead + (subs - ahead) // 2, subs):
            direct(0, k)
    for j in range(cols // chunk):
        w_rest(j)
    def all_direct(j, carry):
        for k in range(subs):
            direct(j, k)
        return carry

    lax.fori_loop(1 if whole_blocks else 0, half - 1, all_direct, 0)
    w_two[q_hi, :, :] = part(dw_ref, me_q, k_piece)[...] + w_one[q_hi]
    for k in range(subs):
        feat_two[hi, pl.ds(k * sub, sub), :] = feat_add(hi, k)

    wait_all(dots, n_patch, col_send.at[ITERS], col_recv.at[ITERS])
    await_bytes(w_two.at[pl.ds(0, q_half - 1)], w_sem.at[3])
    wait_rows(CROSS)
    loss_ref[...] = jnp.log(totals) - 10.0 * jnp.sum(row_buf[CROSS], axis=0) * b_row
    dot = jnp.sum(col_buf[ITERS], axis=0)
    r_w = rw_ref[...]
    w_mine = part(proto_ref, me_q, k_piece)[...].astype(F32)
    gp_ref[...] = r_w * jnp.sum(w_two[...], axis=0) - w_mine * (r_w * r_w * r_w * dot)

    if ahead:
        outer = jnp.logical_or(hi == 0, hi == half - 1)

        @pl.when(outer)
        def _():
            for out in range(2):
                await_bytes(early_buf.at[out], early_sem.at[out, 1])
            top = pl.ds(pl.multiple_of(me_p * piece, piece), head)
            a_part = t_ref[top, :] * jnp.sum(early_buf[0], axis=0)
            b_part = b_ref[top, :] * jnp.sum(early_buf[1], axis=0)
            source = 2 * (1 - upper)
            feat_two[source, pl.ds(0, head), :] = a_part
            feat_two[source + 1, pl.ds(0, head), :] = -b_part
            await_bytes(feat_two.at[pl.ds(0, 2)], feat_two_sem.at[1])

        @pl.when(jnp.logical_not(outer))
        def _():
            await_bytes(feat_two.at[pl.ds(0, 3)], feat_two_sem.at[1])

    else:
        await_bytes(feat_two.at[pl.ds(0, half - 1)], feat_two_sem.at[1])
    x = part(rows_ref, me_p, piece)[...]
    g = jnp.sum(feat_two[...], axis=0)
    r = lax.rsqrt(jnp.sum(x * x, axis=1, keepdims=True) + 1e-12)
    gs_ref[...] = r * g - x * (r * r * r * jnp.sum(x * g, axis=1, keepdims=True))

    await_bytes(w_one, w_sem.at[0])
    await_bytes(w_two.at[pl.ds(0, q_half - 1)], w_sem.at[2])
    await_bytes(feat_zero, feat_zero_sem.at[0])
    await_bytes(feat_one, feat_one_send)
    if ahead:
        for out in range(2):
            await_bytes(early_buf.at[out, 0], early_sem.at[out, 0])
        await_bytes(feat_two.at[0, pl.ds(0, piece - head), :], feat_two_sem.at[0])
        await_bytes(feat_two.at[pl.ds(0, half - 2)], feat_two_sem.at[0])
    else:
        await_bytes(feat_two.at[pl.ds(0, half - 1)], feat_two_sem.at[0])


def finish(loss_in, gs_in, gp_in, loss_ref, gs_ref, gp_ref):
    loss_ref[...] = loss_in[...].reshape(loss_ref.shape)
    gs_ref[...] = gs_in[...]
    gp_ref[...] = gp_in[...]


def solution(mesh):
    n_proto, n_patch = mesh.shape["proto"], mesh.shape["patch"]

    def shards(teacher_feats, student_feats, masked, progress_counter, prototypes):
        images, slots = masked.shape
        rows = images * slots
        width, cols = prototypes.shape
        piece, k_piece = rows // n_proto, width // n_patch
        subs = SUBS if piece % (8 * SUBS) == 0 else 1
        vmem = pl.BlockSpec(memory_space=pltpu.VMEM)
        held = pl.pallas_call(
            functools.partial(kernel, n_proto, n_patch),
            out_shape=(
                pltpu.VMEM((1, rows), F32),
                pltpu.VMEM((piece, width), F32),
                pltpu.VMEM((k_piece, cols), F32),
            ),
            in_specs=[pl.BlockSpec(memory_space=pltpu.HBM)] * 5,
            out_specs=(vmem, vmem, vmem),
            scratch_shapes=[
                pltpu.VMEM((1, 1), jnp.int32),
                pltpu.VMEM(teacher_feats.shape, BF16),
                pltpu.VMEM(student_feats.shape, BF16),
                pltpu.VMEM(masked.shape, jnp.int32),
                pltpu.VMEM(prototypes.shape, BF16),
                pltpu.VMEM((1, cols), F32),
                pltpu.SemaphoreType.DMA((5,)),
                pltpu.VMEM((width, cols), BF16),
                pltpu.VMEM((rows, cols), F32),
                pltpu.VMEM((rows, cols), F32),
                pltpu.VMEM((rows, cols), F32),
                pltpu.VMEM((rows, cols), BF16),
                pltpu.VMEM((rows, width), F32),
                pltpu.VMEM((width, rows), BF16),
                pltpu.VMEM((rows, width), F32),
                pltpu.VMEM((width, cols), F32),
                pltpu.VMEM((rows, width), BF16),
                pltpu.VMEM((rows, width), BF16),
                pltpu.VMEM((1, cols), F32),
                pltpu.VMEM((rows, width), F32),
                pltpu.VMEM((rows, 1), F32),
                pltpu.VMEM((rows, 1), F32),
                pltpu.VMEM((n_proto // 2, piece, width), F32),
                pltpu.SemaphoreType.DMA((3,)),
                pltpu.VMEM((ITERS + 1, n_patch, 1, cols), F32),
                pltpu.VMEM((ITERS + 2, n_proto, 1, rows), F32),
                pltpu.VMEM((n_proto // 2, piece, width), F32),
                pltpu.VMEM((n_proto // 2, piece, width), F32),
                pltpu.VMEM((n_patch // 2, k_piece, cols), F32),
                pltpu.VMEM((n_patch // 2, k_piece, cols), F32),
                pltpu.SemaphoreType.DMA((ITERS + 1,)),
                pltpu.SemaphoreType.DMA((ITERS + 1,)),
                pltpu.SemaphoreType.DMA((ITERS + 2,)),
                pltpu.SemaphoreType.DMA((ITERS + 2,)),
                pltpu.SemaphoreType.DMA,
                pltpu.SemaphoreType.DMA((n_proto // 2, subs)),
                pltpu.SemaphoreType.DMA((2,)),
                pltpu.VMEM((2, 2, max(8, subs // 2 * (piece // subs)), width), F32),
                pltpu.SemaphoreType.DMA((2, 2)),
                pltpu.SemaphoreType.DMA((4,)),
                pltpu.SemaphoreType.DMA((4,)),
            ],
            compiler_params=pltpu.CompilerParams(
                collective_id=0, has_side_effects=True, vmem_limit_bytes=VLIM << 20
            ),
        )(progress_counter.reshape(1, 1), teacher_feats, student_feats, masked, prototypes)
        return tuple(
            pl.pallas_call(
                finish,
                out_shape=(
                    jax.ShapeDtypeStruct((rows,), F32),
                    jax.ShapeDtypeStruct((piece, width), F32),
                    jax.ShapeDtypeStruct((k_piece, cols), F32),
                ),
                in_specs=[vmem] * 3,
                out_specs=(vmem,) * 3,
            )(*(pltpu.with_memory_space_constraint(x, pltpu.VMEM) for x in held))
        )

    in_specs = (P("patch", None), P("patch", None), P("patch", None), P(), P(None, "proto"))
    out_specs = (P("patch"), P(("patch", "proto"), None), P("patch", "proto"))
    return jax.shard_map(shards, mesh=mesh, in_specs=in_specs, out_specs=out_specs, check_vma=False)
```

```python
import functools

import jax
import jax.numpy as jnp
from jax import lax
from jax.experimental import pallas as pl
from jax.experimental.pallas import tpu as pltpu
from jax.sharding import PartitionSpec as P

ITERS = 3
HEATUP_LENGTH = 30
LOG2E = 1.4426950408889634
MESH = pl.DeviceIdType.MESH
F32 = jnp.float32
BF16 = jnp.bfloat16
U_T, U_S, U_P, U_G = 4, 2, 8, 4
TILE, RB = 256, 256
SUBS = 4
TOTAL, CROSS = ITERS, ITERS + 1
VLIM = 62
NT = (((1,), (1,)), ((), ()))


def diagonal(size):
    return lax.broadcasted_iota(jnp.int32, (size, size), 0) == lax.broadcasted_iota(
        jnp.int32, (size, size), 1
    )


def to_row(column, eye):
    return jnp.sum(jnp.where(eye, column, 0.0), axis=0, keepdims=True)


def to_column(row, eye):
    return jnp.sum(jnp.where(eye, row, 0.0), axis=1, keepdims=True)


def remote(src, dst, send, recv, axis, peer):
    return pltpu.make_async_remote_copy(
        src_ref=src,
        dst_ref=dst,
        send_sem=send,
        recv_sem=recv,
        device_id={axis: peer},
        device_id_type=MESH,
    )


def await_bytes(ref, sem):
    pltpu.make_async_copy(ref, ref, sem).wait()


def kernel(
    n_proto,
    n_patch,
    progress_hbm,
    teacher_hbm,
    student_hbm,
    masked_hbm,
    proto_hbm,
    loss_ref,
    gs_ref,
    gp_ref,
    progress_ref,
    teacher_ref,
    student_ref,
    masked_ref,
    proto_ref,
    rw_ref,
    load_sem,
    w_hat,
    e_ref,
    s_ref,
    p_ref,
    g_ref,
    rows_ref,
    shat_t,
    ds_ref,
    dw_ref,
    t_hat,
    s_hat,
    sharp_ref,
    da_ref,
    t_ref,
    b_ref,
    feat_zero,
    feat_zero_sem,
    col_buf,
    row_buf,
    feat_one,
    feat_two,
    w_one,
    w_two,
    col_send,
    col_recv,
    row_send,
    row_recv,
    feat_one_send,
    feat_one_recv,
    feat_two_sem,
    early_buf,
    early_sem,
    w_one_recv,
    w_sem,
):
    me_p = lax.axis_index("proto")
    me_q = lax.axis_index("patch")
    images, slots = masked_ref.shape
    per_image = teacher_ref.shape[0] // images
    width, cols = proto_ref.shape
    rows = images * slots
    chunk = cols // 4

    loads = [
        pltpu.make_async_copy(src, dst, load_sem.at[k])
        for k, (src, dst) in enumerate(
            (
                (proto_hbm, proto_ref),
                (masked_hbm, masked_ref),
                (progress_hbm, progress_ref),
                (teacher_hbm, teacher_ref),
                (student_hbm, student_ref),
            )
        )
    ]
    for load in loads:
        load.start()

    barrier = pltpu.get_barrier_semaphore()

    def greet(axis, me, n):
        def body(d, carry):
            pl.semaphore_signal(
                barrier, inc=1, device_id={axis: lax.rem(me + d, n)}, device_id_type=MESH
            )
            return carry

        lax.fori_loop(1, n, body, 0)

    greet("proto", me_p, n_proto)
    greet("patch", me_q, n_patch)

    eye = diagonal(slots)
    lane = lax.broadcasted_iota(jnp.int32, (slots, per_image), 1)

    def block(i):
        return pl.ds(pl.multiple_of(i * slots, slots), slots)

    def gathered(ref, i):
        picks = masked_ref[pl.ds(i, 1), :]
        picks = jnp.sum(jnp.where(eye, picks, 0), axis=1, keepdims=True)
        hot = jnp.where(picks == lane, 1.0, 0.0).astype(BF16)
        at = pl.ds(pl.multiple_of(i * per_image, per_image), per_image)
        return jnp.dot(hot, ref[at, :], preferred_element_type=F32)

    def unit(x):
        return x * lax.rsqrt(jnp.sum(x * x, axis=1, keepdims=True) + 1e-12)

    def folded(x):
        return jnp.sum(x.reshape(slots // 8, 8, cols), axis=0)

    loads[0].wait()
    w_raw = proto_ref[...].astype(F32)
    r_w = lax.rsqrt(jnp.sum(w_raw * w_raw, axis=0, keepdims=True) + 1e-12)
    rw_ref[...] = r_w
    w_hat[...] = (w_raw * r_w).astype(BF16)

    loads[2].wait()
    steps = jnp.broadcast_to(progress_ref[...].astype(F32), (1, cols))
    sharp_ref[...] = LOG2E / (0.04 + 0.03 * steps / HEATUP_LENGTH)

    def teacher_rows(i, carry):
        t_hat[block(i), :] = unit(gathered(teacher_ref, i)).astype(BF16)
        return carry

    def teacher_tile(j, carry):
        at = pl.ds(pl.multiple_of(j * TILE, TILE), TILE)
        total = None
        for k in range(rows // RB):
            here = pl.ds(k * RB, RB)
            e = jnp.dot(t_hat[here, :], w_hat[:, at], preferred_element_type=F32)
            e = jnp.exp2(e * sharp_ref[:, at])
            e_ref[here, at] = e
            part_sum = jnp.sum(e.reshape(RB // 8, 8, TILE), axis=0)
            total = part_sum if total is None else total + part_sum
        col_buf[0, me_q, :, at] = jnp.sum(total, axis=0, keepdims=True)
        return carry

    def student_rows(i, carry):
        x = gathered(student_ref, i)
        rows_ref[block(i), :] = x
        s_unit = unit(x)
        s_hat[block(i), :] = s_unit.astype(BF16)
        shat_t[:, block(i)] = s_unit.T.astype(BF16)
        return carry

    def student_block(i, carry):
        s = jnp.dot(s_hat[block(i), :], w_hat[...], preferred_element_type=F32)
        s_ref[block(i), :] = s
        p = jnp.exp2(s * (10.0 * LOG2E))
        p_ref[block(i), :] = p
        total = jnp.sum(p, axis=1, keepdims=True)
        row_buf[TOTAL, me_p, :, block(i)] = to_row(total, eye)
        return carry

    def spread(x):
        high = x.astype(BF16)
        low = (x - high.astype(F32)).astype(BF16)
        both = jnp.concatenate([high, low], axis=0)
        out = lax.dot_general(both, w_hat[...], NT, preferred_element_type=F32)
        return out[:slots] + out[slots:]

    def a_block(i, carry):
        da_ref[block(i), :] = spread(p_ref[block(i), :])
        return carry

    def b_block(i, carry):
        ds_ref[block(i), :] = spread(e_ref[block(i), :])
        return carry

    def send_all(buf, axis, me, n, send, recv):
        def body(k, carry):
            peer = jnp.bitwise_xor(me, n - 1 - k)
            remote(buf.at[me], buf.at[me], send, recv, axis, peer).start()
            return carry

        lax.fori_loop(0, n - 1, body, 0, unroll=n <= 8)

    def wait_all(buf, n, send, recv):
        await_bytes(buf.at[pl.ds(0, n - 1)], recv)
        await_bytes(buf.at[pl.ds(0, n - 1)], send)

    def column_pass(b_row_at, acc0):
        def body(i, acc):
            b_col = to_column(b_row_at(i), eye)
            return acc + folded(e_ref[block(i), :] * b_col)

        return lax.fori_loop(0, images, body, acc0, unroll=U_P)

    half = n_proto // 2
    hi, lo = me_p // 2, lax.rem(me_p, 2)
    other = 1 - lo
    piece = rows // n_proto
    whole_blocks = n_proto == images
    subs = feat_one_recv.shape[1]
    sub = piece // subs
    ahead = subs // 2 if whole_blocks and half == 4 else 0
    head = ahead * sub
    upper = (2 * hi) // half

    def far_first(j):
        down = half - 1 - j - (j + hi + 1) // half
        up = j + (j + half - hi) // half
        return (1 - upper) * down + upper * up

    def place(j):
        return far_first(j) if j < half - 1 else hi

    def part(ref, o, size):
        return ref.at[pl.ds(pl.multiple_of(o * size, size), size), :]

    def a_pair(o_hi, at=1):
        remote(
            part(da_ref, o_hi * 2 + other, piece),
            feat_zero.at[o_hi],
            feat_zero_sem.at[0],
            feat_zero_sem.at[at],
            "proto",
            hi * 2 + other,
        ).start()

    def sub_part(ref, o, k):
        return ref.at[pl.ds(pl.multiple_of(o * piece + k * sub, sub), sub), :]

    def sub_slot(ref, o_hi, k):
        return ref.at[o_hi, pl.ds(k * sub, sub), :]

    def b_pair(o_hi):
        for k in range(subs):
            remote(
                sub_part(ds_ref, o_hi * 2 + other, k),
                sub_slot(feat_one, o_hi, k),
                feat_one_send,
                feat_one_recv.at[o_hi, k],
                "proto",
                hi * 2 + other,
            ).start()

    def early(ref, got, out, k):
        o_hi = place(0)
        mine = sub_part(ref, o_hi * 2 + lo, k)
        mine[...] = mine[...] + got[o_hi, pl.ds(k * sub, sub), :]
        remote(
            mine,
            early_buf.at[out, lax.rem(hi, 2), pl.ds(k * sub, sub), :],
            early_sem.at[out, 0],
            early_sem.at[out, 1],
            "proto",
            o_hi * 2 + lo,
        ).start()

    def each(n, f):
        def body(j, carry):
            f(j)
            return carry

        lax.fori_loop(0, n, body, 0)

    zero = jnp.zeros((8, cols), F32)
    loads[1].wait()
    loads[3].wait()
    lax.fori_loop(0, images, teacher_rows, 0, unroll=True)
    lax.fori_loop(0, cols // TILE, teacher_tile, 0, unroll=U_T)
    loads[4].wait()
    pl.semaphore_wait(barrier, n_proto + n_patch - 2)

    def send_rows(k):
        send_all(row_buf.at[k], "proto", me_p, n_proto, row_send.at[k], row_recv.at[k])

    def wait_rows(k):
        wait_all(row_buf.at[k], n_proto, row_send.at[k], row_recv.at[k])

    def send_cols(k):
        send_all(col_buf.at[k], "patch", me_q, n_patch, col_send.at[k], col_recv.at[k])

    def wait_cols(k):
        wait_all(col_buf.at[k], n_patch, col_send.at[k], col_recv.at[k])

    def row_pass(it):
        a_row = 1.0 / jnp.sum(col_buf[it], axis=0)

        def body(i, carry):
            ea = e_ref[block(i), :] * a_row
            if it + 1 == ITERS:
                e_ref[block(i), :] = ea
            row_buf[it, me_p, :, block(i)] = to_row(jnp.sum(ea, axis=1, keepdims=True), eye)
            return carry

        if it + 1 == ITERS and whole_blocks:
            at = block(2 * place(0) + other)
            ds_ref[at, :] = spread(e_ref[at, :] * a_row)
        lax.fori_loop(0, images, body, 0, unroll=U_P)
        send_rows(it)

    def col_pass(it):
        loss_ref[...] = 1.0 / jnp.sum(row_buf[it], axis=0)
        acc = column_pass(lambda i: loss_ref[:, block(i)], zero)
        col_buf[it + 1, me_q, :, :] = jnp.sum(acc, axis=0, keepdims=True)
        send_cols(it + 1)

    send_cols(0)
    lax.fori_loop(0, images, student_rows, 0, unroll=U_S)
    if whole_blocks:
        student_block(2 * place(0) + other, 0)
    wait_cols(0)

    row_pass(0)
    if whole_blocks:
        a_block(2 * place(0) + other, 0)
        a_pair(place(0), 2 if ahead else 1)
        student_block(2 * place(1) + other, 0)
        a_block(2 * place(1) + other, 0)
        a_pair(place(1))
        for j in range(2, half):
            student_block(2 * place(j) + other, 0)
        student_block(lo, 0)
    else:
        lax.fori_loop(0, images, student_block, 0, unroll=U_S)
    wait_rows(0)
    col_pass(0)
    if whole_blocks:
        for j in range(1, half):
            student_block(2 * j + lo, 0)
    wait_cols(1)

    row_pass(1)
    send_rows(TOTAL)
    if whole_blocks:
        for j in range(2, half):
            a_block(2 * place(j) + other, 0)
            a_pair(place(j))
        for j in range(half):
            a_block(2 * j + lo, 0)
    else:
        lax.fori_loop(0, images, a_block, 0, unroll=U_S)
        each(half, a_pair)
    wait_rows(1)
    col_pass(1)

    if ahead:
        await_bytes(feat_zero.at[place(0)], feat_zero_sem.at[2])
        for k in range(ahead):
            early(da_ref, feat_zero, 0, k)
    wait_rows(TOTAL)
    totals = jnp.sum(row_buf[TOTAL], axis=0)
    scale = 1.0 / (0.1 * rows * n_patch)
    col_buf[0, 1, :, :] = scale / totals

    def weigh(i, carry):
        t_col = to_column(col_buf[0, 1, :, block(i)], eye)
        t_ref[block(i), :] = t_col
        p_ref[block(i), :] = p_ref[block(i), :] * t_col
        return carry

    lax.fori_loop(0, images, weigh, 0, unroll=U_S)
    wait_cols(2)

    row_pass(2)

    def cross_body(i, carry):
        x = jnp.sum(e_ref[block(i), :] * s_ref[block(i), :], axis=1, keepdims=True)
        row_buf[CROSS, me_p, :, block(i)] = to_row(x, eye)
        return carry

    def cross():
        lax.fori_loop(0, images, cross_body, 0, unroll=U_S)
        send_rows(CROSS)

    if whole_blocks:
        for j in range(half):
            if j:
                b_block(2 * place(j) + other, 0)
            b_pair(place(j))
            if j == 0:
                cross()
        for j in range(half):
            b_block(2 * place(j) + lo, 0)
    else:
        lax.fori_loop(0, images, b_block, 0, unroll=U_S)
        cross()
        each(half, b_pair)

    def join(g):
        mine = part(da_ref, 2 * g + lo, piece)
        mine[...] = (mine[...] + feat_zero[g]) * part(t_ref, 2 * g + lo, piece)[...]

    if ahead:
        await_bytes(feat_zero.at[pl.ds(0, half - 1)], feat_zero_sem.at[1])
        for k in range(ahead, subs):
            mine = sub_part(da_ref, 2 * place(0) + lo, k)
            got = feat_zero[place(0), pl.ds(k * sub, sub), :]
            mine[...] = (mine[...] + got) * sub_part(t_ref, 2 * place(0) + lo, k)[...]
        for j in range(1, half):
            join(place(j))
        for k in range(ahead):
            await_bytes(sub_slot(feat_one, place(0), k), feat_one_recv.at[place(0), k])
            early(ds_ref, feat_one, 1, k)
    else:
        await_bytes(feat_zero, feat_zero_sem.at[1])
        each(half, join)
    wait_rows(2)
    b_row = 1.0 / jnp.sum(row_buf[2], axis=0)
    col_buf[0, 0, :, :] = b_row * scale

    def to_b(i, carry):
        b_ref[block(i), :] = to_column(col_buf[0, 0, :, block(i)], eye)
        return carry

    lax.fori_loop(0, images, to_b, 0, unroll=U_P)

    def feat_add(o_hi, k):
        await_bytes(sub_slot(feat_one, o_hi, k), feat_one_recv.at[o_hi, k])
        o = o_hi * 2 + lo
        both = sub_part(ds_ref, o, k)[...] + feat_one[o_hi, pl.ds(k * sub, sub), :]
        return sub_part(da_ref, o, k)[...] - sub_part(b_ref, o, k)[...] * both

    def feat_send(o_hi, k):
        remote(
            sub_part(da_ref, o_hi * 2 + lo, k),
            sub_slot(feat_two, hi, k),
            feat_two_sem.at[0],
            feat_two_sem.at[1],
            "proto",
            o_hi * 2 + lo,
        ).start()

    def direct(j, k):
        o_hi = far_first(j)
        sub_part(da_ref, o_hi * 2 + lo, k)[...] = feat_add(o_hi, k)
        feat_send(o_hi, k)

    k_piece = width // n_patch
    q_half = n_patch // 2
    q_hi, q_lo = me_q // 2, lax.rem(me_q, 2)
    q_other = 1 - q_lo

    def w_slab(ref, o, j):
        return ref.at[
            pl.ds(pl.multiple_of(o * k_piece, k_piece), k_piece), pl.ds(j * chunk, chunk)
        ]

    def dw_chunk(j):
        at = pl.ds(j * chunk, chunk)
        g = (p_ref[:, at] - e_ref[:, at] * b_ref[...]).astype(BF16)
        dw = jnp.dot(shat_t[...], g, preferred_element_type=F32)
        dw_ref[:, at] = dw

        def w_pair(d, carry):
            o_hi = lax.rem(q_hi + d, q_half)
            remote(
                w_slab(dw_ref, o_hi * 2 + q_other, j),
                w_one.at[o_hi, :, at],
                w_sem.at[0],
                w_one_recv.at[j],
                "patch",
                q_hi * 2 + q_other,
            ).start()
            return carry

        lax.fori_loop(1, q_half + 1, w_pair, 0)
        col_buf[ITERS, me_q, :, at] = jnp.sum(
            dw * proto_ref[:, at].astype(F32), axis=0, keepdims=True
        )

    def w_rest(j):
        at = pl.ds(j * chunk, chunk)
        await_bytes(w_one.at[:, :, at], w_one_recv.at[j])

        def body(d, carry):
            o_hi = lax.rem(q_hi + d, q_half)
            mine = w_slab(dw_ref, o_hi * 2 + q_lo, j)
            mine[...] = mine[...] + w_one[o_hi, :, at]
            remote(
                mine,
                w_two.at[q_hi, :, at],
                w_sem.at[2],
                w_sem.at[3],
                "patch",
                o_hi * 2 + q_lo,
            ).start()
            return carry

        lax.fori_loop(1, q_half, body, 0)

    if whole_blocks:
        for k in range(ahead, ahead + (subs - ahead) // 2):
            direct(0, k)
    for j in range(cols // chunk):
        dw_chunk(j)
    dots = col_buf.at[ITERS]
    send_cols(ITERS)
    if whole_blocks:
        for k in range(ahead + (subs - ahead) // 2, subs):
            direct(0, k)
    for j in range(cols // chunk):
        w_rest(j)
    def all_direct(j, carry):
        for k in range(subs):
            direct(j, k)
        return carry

    lax.fori_loop(1 if whole_blocks else 0, half - 1, all_direct, 0)
    w_two[q_hi, :, :] = part(dw_ref, me_q, k_piece)[...] + w_one[q_hi]
    for k in range(subs):
        feat_two[hi, pl.ds(k * sub, sub), :] = feat_add(hi, k)

    wait_all(dots, n_patch, col_send.at[ITERS], col_recv.at[ITERS])
    await_bytes(w_two.at[pl.ds(0, q_half - 1)], w_sem.at[3])
    wait_rows(CROSS)
    loss_ref[...] = jnp.log(totals) - 10.0 * jnp.sum(row_buf[CROSS], axis=0) * b_row
    dot = jnp.sum(col_buf[ITERS], axis=0)
    r_w = rw_ref[...]
    w_mine = part(proto_ref, me_q, k_piece)[...].astype(F32)
    gp_ref[...] = r_w * jnp.sum(w_two[...], axis=0) - w_mine * (r_w * r_w * r_w * dot)

    if ahead:
        outer = jnp.logical_or(hi == 0, hi == half - 1)

        @pl.when(outer)
        def _():
            for out in range(2):
                await_bytes(early_buf.at[out], early_sem.at[out, 1])
            top = pl.ds(pl.multiple_of(me_p * piece, piece), head)
            a_part = t_ref[top, :] * jnp.sum(early_buf[0], axis=0)
            b_part = b_ref[top, :] * jnp.sum(early_buf[1], axis=0)
            source = 2 * (1 - upper)
            feat_two[source, pl.ds(0, head), :] = a_part
            feat_two[source + 1, pl.ds(0, head), :] = -b_part
            await_bytes(feat_two.at[pl.ds(0, 2)], feat_two_sem.at[1])

        @pl.when(jnp.logical_not(outer))
        def _():
            await_bytes(feat_two.at[pl.ds(0, 3)], feat_two_sem.at[1])

    else:
        await_bytes(feat_two.at[pl.ds(0, half - 1)], feat_two_sem.at[1])
    x = part(rows_ref, me_p, piece)[...]
    g = jnp.sum(feat_two[...], axis=0)
    r = lax.rsqrt(jnp.sum(x * x, axis=1, keepdims=True) + 1e-12)
    gs_ref[...] = r * g - x * (r * r * r * jnp.sum(x * g, axis=1, keepdims=True))

    await_bytes(w_one, w_sem.at[0])
    await_bytes(w_two.at[pl.ds(0, q_half - 1)], w_sem.at[2])
    await_bytes(feat_zero, feat_zero_sem.at[0])
    await_bytes(feat_one, feat_one_send)
    if ahead:
        for out in range(2):
            await_bytes(early_buf.at[out, 0], early_sem.at[out, 0])
        await_bytes(feat_two.at[0, pl.ds(0, piece - head), :], feat_two_sem.at[0])
        await_bytes(feat_two.at[pl.ds(0, half - 2)], feat_two_sem.at[0])
    else:
        await_bytes(feat_two.at[pl.ds(0, half - 1)], feat_two_sem.at[0])


def finish(loss_in, gs_in, gp_in, loss_ref, gs_ref, gp_ref):
    loss_ref[...] = loss_in[...].reshape(loss_ref.shape)
    gs_ref[...] = gs_in[...]
    gp_ref[...] = gp_in[...]


def solution(mesh):
    n_proto, n_patch = mesh.shape["proto"], mesh.shape["patch"]

    def shards(teacher_feats, student_feats, masked, progress_counter, prototypes):
        images, slots = masked.shape
        rows = images * slots
        width, cols = prototypes.shape
        piece, k_piece = rows // n_proto, width // n_patch
        subs = SUBS if piece % (8 * SUBS) == 0 else 1
        vmem = pl.BlockSpec(memory_space=pltpu.VMEM)
        held = pl.pallas_call(
            functools.partial(kernel, n_proto, n_patch),
            out_shape=(
                pltpu.VMEM((1, rows), F32),
                pltpu.VMEM((piece, width), F32),
                pltpu.VMEM((k_piece, cols), F32),
            ),
            in_specs=[pl.BlockSpec(memory_space=pltpu.HBM)] * 5,
            out_specs=(vmem, vmem, vmem),
            scratch_shapes=[
                pltpu.VMEM((1, 1), jnp.int32),
                pltpu.VMEM(teacher_feats.shape, BF16),
                pltpu.VMEM(student_feats.shape, BF16),
                pltpu.VMEM(masked.shape, jnp.int32),
                pltpu.VMEM(prototypes.shape, BF16),
                pltpu.VMEM((1, cols), F32),
                pltpu.SemaphoreType.DMA((5,)),
                pltpu.VMEM((width, cols), BF16),
                pltpu.VMEM((rows, cols), F32),
                pltpu.VMEM((rows, cols), F32),
                pltpu.VMEM((rows, cols), F32),
                pltpu.VMEM((rows, cols), BF16),
                pltpu.VMEM((rows, width), F32),
                pltpu.VMEM((width, rows), BF16),
                pltpu.VMEM((rows, width), F32),
                pltpu.VMEM((width, cols), F32),
                pltpu.VMEM((rows, width), BF16),
                pltpu.VMEM((rows, width), BF16),
                pltpu.VMEM((1, cols), F32),
                pltpu.VMEM((rows, width), F32),
                pltpu.VMEM((rows, 1), F32),
                pltpu.VMEM((rows, 1), F32),
                pltpu.VMEM((n_proto // 2, piece, width), F32),
                pltpu.SemaphoreType.DMA((3,)),
                pltpu.VMEM((ITERS + 1, n_patch, 1, cols), F32),
                pltpu.VMEM((ITERS + 2, n_proto, 1, rows), F32),
                pltpu.VMEM((n_proto // 2, piece, width), F32),
                pltpu.VMEM((n_proto // 2, piece, width), F32),
                pltpu.VMEM((n_patch // 2, k_piece, cols), F32),
                pltpu.VMEM((n_patch // 2, k_piece, cols), F32),
                pltpu.SemaphoreType.DMA((ITERS + 1,)),
                pltpu.SemaphoreType.DMA((ITERS + 1,)),
                pltpu.SemaphoreType.DMA((ITERS + 2,)),
                pltpu.SemaphoreType.DMA((ITERS + 2,)),
                pltpu.SemaphoreType.DMA,
                pltpu.SemaphoreType.DMA((n_proto // 2, subs)),
                pltpu.SemaphoreType.DMA((2,)),
                pltpu.VMEM((2, 2, max(8, subs // 2 * (piece // subs)), width), F32),
                pltpu.SemaphoreType.DMA((2, 2)),
                pltpu.SemaphoreType.DMA((4,)),
                pltpu.SemaphoreType.DMA((4,)),
            ],
            compiler_params=pltpu.CompilerParams(
                collective_id=0, has_side_effects=True, vmem_limit_bytes=VLIM << 20
            ),
        )(progress_counter.reshape(1, 1), teacher_feats, student_feats, masked, prototypes)
        return tuple(
            pl.pallas_call(
                finish,
                out_shape=(
                    jax.ShapeDtypeStruct((rows,), F32),
                    jax.ShapeDtypeStruct((piece, width), F32),
                    jax.ShapeDtypeStruct((k_piece, cols), F32),
                ),
                in_specs=[vmem] * 3,
                out_specs=(vmem,) * 3,
            )(*(pltpu.with_memory_space_constraint(x, pltpu.VMEM) for x in held))
        )

    in_specs = (P("patch", None), P("patch", None), P("patch", None), P(), P(None, "proto"))
    out_specs = (P("patch"), P(("patch", "proto"), None), P("patch", "proto"))
    return jax.shard_map(shards, mesh=mesh, in_specs=in_specs, out_specs=out_specs, check_vma=False)
```

```python
import functools

import jax
import jax.numpy as jnp
from jax import lax
from jax.experimental import pallas as pl
from jax.experimental.pallas import tpu as pltpu
from jax.sharding import PartitionSpec as P

ITERS = 3
HEATUP_LENGTH = 30
LOG2E = 1.4426950408889634
MESH = pl.DeviceIdType.MESH
F32 = jnp.float32
BF16 = jnp.bfloat16
U_T, U_S, U_P, U_G = 4, 2, 8, 4
TILE, RB = 256, 256
SUBS = 4
TOTAL, CROSS = ITERS, ITERS + 1
VLIM = 62
NT = (((1,), (1,)), ((), ()))


def diagonal(size):
    return lax.broadcasted_iota(jnp.int32, (size, size), 0) == lax.broadcasted_iota(
        jnp.int32, (size, size), 1
    )


def to_row(column, eye):
    return jnp.sum(jnp.where(eye, column, 0.0), axis=0, keepdims=True)


def to_column(row, eye):
    return jnp.sum(jnp.where(eye, row, 0.0), axis=1, keepdims=True)


def remote(src, dst, send, recv, axis, peer):
    return pltpu.make_async_remote_copy(
        src_ref=src,
        dst_ref=dst,
        send_sem=send,
        recv_sem=recv,
        device_id={axis: peer},
        device_id_type=MESH,
    )


def await_bytes(ref, sem):
    pltpu.make_async_copy(ref, ref, sem).wait()


def kernel(
    n_proto,
    n_patch,
    progress_hbm,
    teacher_hbm,
    student_hbm,
    masked_hbm,
    proto_hbm,
    loss_ref,
    gs_ref,
    gp_ref,
    progress_ref,
    teacher_ref,
    student_ref,
    masked_ref,
    proto_ref,
    rw_ref,
    load_sem,
    w_hat,
    e_ref,
    s_ref,
    p_ref,
    g_ref,
    rows_ref,
    shat_t,
    ds_ref,
    dw_ref,
    t_hat,
    s_hat,
    sharp_ref,
    da_ref,
    t_ref,
    b_ref,
    feat_zero,
    feat_zero_sem,
    col_buf,
    row_buf,
    feat_one,
    feat_two,
    w_one,
    w_two,
    col_send,
    col_recv,
    row_send,
    row_recv,
    feat_one_send,
    feat_one_recv,
    feat_two_sem,
    early_buf,
    early_sem,
    w_one_recv,
    w_sem,
):
    me_p = lax.axis_index("proto")
    me_q = lax.axis_index("patch")
    images, slots = masked_ref.shape
    per_image = teacher_ref.shape[0] // images
    width, cols = proto_ref.shape
    rows = images * slots
    chunk = cols // 4

    loads = [
        pltpu.make_async_copy(src, dst, load_sem.at[k])
        for k, (src, dst) in enumerate(
            (
                (proto_hbm, proto_ref),
                (masked_hbm, masked_ref),
                (progress_hbm, progress_ref),
                (teacher_hbm, teacher_ref),
                (student_hbm, student_ref),
            )
        )
    ]
    for load in loads:
        load.start()

    barrier = pltpu.get_barrier_semaphore()

    def greet(axis, me, n):
        def body(d, carry):
            pl.semaphore_signal(
                barrier, inc=1, device_id={axis: lax.rem(me + d, n)}, device_id_type=MESH
            )
            return carry

        lax.fori_loop(1, n, body, 0)

    greet("proto", me_p, n_proto)
    greet("patch", me_q, n_patch)

    eye = diagonal(slots)
    lane = lax.broadcasted_iota(jnp.int32, (slots, per_image), 1)

    def block(i):
        return pl.ds(pl.multiple_of(i * slots, slots), slots)

    def gathered(ref, i):
        picks = masked_ref[pl.ds(i, 1), :]
        picks = jnp.sum(jnp.where(eye, picks, 0), axis=1, keepdims=True)
        hot = jnp.where(picks == lane, 1.0, 0.0).astype(BF16)
        at = pl.ds(pl.multiple_of(i * per_image, per_image), per_image)
        return jnp.dot(hot, ref[at, :], preferred_element_type=F32)

    def unit(x):
        return x * lax.rsqrt(jnp.sum(x * x, axis=1, keepdims=True) + 1e-12)

    def folded(x):
        return jnp.sum(x.reshape(slots // 8, 8, cols), axis=0)

    loads[0].wait()
    w_raw = proto_ref[...].astype(F32)
    r_w = lax.rsqrt(jnp.sum(w_raw * w_raw, axis=0, keepdims=True) + 1e-12)
    rw_ref[...] = r_w
    w_hat[...] = (w_raw * r_w).astype(BF16)

    loads[2].wait()
    steps = jnp.broadcast_to(progress_ref[...].astype(F32), (1, cols))
    sharp_ref[...] = LOG2E / (0.04 + 0.03 * steps / HEATUP_LENGTH)

    def teacher_rows(i, carry):
        t_hat[block(i), :] = unit(gathered(teacher_ref, i)).astype(BF16)
        return carry

    def teacher_tile(j, carry):
        at = pl.ds(pl.multiple_of(j * TILE, TILE), TILE)
        total = None
        for k in range(rows // RB):
            here = pl.ds(k * RB, RB)
            e = jnp.dot(t_hat[here, :], w_hat[:, at], preferred_element_type=F32)
            e = jnp.exp2(e * sharp_ref[:, at])
            e_ref[here, at] = e
            part_sum = jnp.sum(e.reshape(RB // 8, 8, TILE), axis=0)
            total = part_sum if total is None else total + part_sum
        col_buf[0, me_q, :, at] = jnp.sum(total, axis=0, keepdims=True)
        return carry

    def student_rows(i, carry):
        x = gathered(student_ref, i)
        rows_ref[block(i), :] = x
        s_unit = unit(x)
        s_hat[block(i), :] = s_unit.astype(BF16)
        shat_t[:, block(i)] = s_unit.T.astype(BF16)
        return carry

    def student_block(i, carry):
        s = jnp.dot(s_hat[block(i), :], w_hat[...], preferred_element_type=F32)
        s_ref[block(i), :] = s
        p = jnp.exp2(s * (10.0 * LOG2E))
        p_ref[block(i), :] = p
        total = jnp.sum(p, axis=1, keepdims=True)
        row_buf[TOTAL, me_p, :, block(i)] = to_row(total, eye)
        return carry

    def spread(x):
        high = x.astype(BF16)
        low = (x - high.astype(F32)).astype(BF16)
        both = jnp.concatenate([high, low], axis=0)
        out = lax.dot_general(both, w_hat[...], NT, preferred_element_type=F32)
        return out[:slots] + out[slots:]

    def a_block(i, carry):
        da_ref[block(i), :] = spread(p_ref[block(i), :])
        return carry

    def b_block(i, carry):
        ds_ref[block(i), :] = spread(e_ref[block(i), :])
        return carry

    def send_all(buf, axis, me, n, send, recv):
        def body(k, carry):
            peer = jnp.bitwise_xor(me, n - 1 - k)
            remote(buf.at[me], buf.at[me], send, recv, axis, peer).start()
            return carry

        lax.fori_loop(0, n - 1, body, 0, unroll=n <= 8)

    def wait_all(buf, n, send, recv):
        await_bytes(buf.at[pl.ds(0, n - 1)], recv)
        await_bytes(buf.at[pl.ds(0, n - 1)], send)

    def column_pass(b_row_at, acc0):
        def body(i, acc):
            b_col = to_column(b_row_at(i), eye)
            return acc + folded(e_ref[block(i), :] * b_col)

        return lax.fori_loop(0, images, body, acc0, unroll=U_P)

    half = n_proto // 2
    hi, lo = me_p // 2, lax.rem(me_p, 2)
    other = 1 - lo
    piece = rows // n_proto
    whole_blocks = n_proto == images
    subs = feat_one_recv.shape[1]
    sub = piece // subs
    ahead = subs // 2 if whole_blocks and half == 4 else 0
    head = ahead * sub
    upper = (2 * hi) // half

    def far_first(j):
        down = half - 1 - j - (j + hi + 1) // half
        up = j + (j + half - hi) // half
        return (1 - upper) * down + upper * up

    def place(j):
        return far_first(j) if j < half - 1 else hi

    def part(ref, o, size):
        return ref.at[pl.ds(pl.multiple_of(o * size, size), size), :]

    def a_pair(o_hi, at=1):
        remote(
            part(da_ref, o_hi * 2 + other, piece),
            feat_zero.at[o_hi],
            feat_zero_sem.at[0],
            feat_zero_sem.at[at],
            "proto",
            hi * 2 + other,
        ).start()

    def sub_part(ref, o, k):
        return ref.at[pl.ds(pl.multiple_of(o * piece + k * sub, sub), sub), :]

    def sub_slot(ref, o_hi, k):
        return ref.at[o_hi, pl.ds(k * sub, sub), :]

    def b_pair(o_hi):
        for k in range(subs):
            remote(
                sub_part(ds_ref, o_hi * 2 + other, k),
                sub_slot(feat_one, o_hi, k),
                feat_one_send,
                feat_one_recv.at[o_hi, k],
                "proto",
                hi * 2 + other,
            ).start()

    def early(ref, got, out, k):
        o_hi = place(0)
        mine = sub_part(ref, o_hi * 2 + lo, k)
        mine[...] = mine[...] + got[o_hi, pl.ds(k * sub, sub), :]
        remote(
            mine,
            early_buf.at[out, lax.rem(hi, 2), pl.ds(k * sub, sub), :],
            early_sem.at[out, 0],
            early_sem.at[out, 1],
            "proto",
            o_hi * 2 + lo,
        ).start()

    def each(n, f):
        def body(j, carry):
            f(j)
            return carry

        lax.fori_loop(0, n, body, 0)

    zero = jnp.zeros((8, cols), F32)
    loads[1].wait()
    loads[3].wait()
    lax.fori_loop(0, images, teacher_rows, 0, unroll=True)
    lax.fori_loop(0, cols // TILE, teacher_tile, 0, unroll=U_T)
    loads[4].wait()
    pl.semaphore_wait(barrier, n_proto + n_patch - 2)

    def send_rows(k):
        send_all(row_buf.at[k], "proto", me_p, n_proto, row_send.at[k], row_recv.at[k])

    def wait_rows(k):
        wait_all(row_buf.at[k], n_proto, row_send.at[k], row_recv.at[k])

    def send_cols(k):
        send_all(col_buf.at[k], "patch", me_q, n_patch, col_send.at[k], col_recv.at[k])

    def wait_cols(k):
        wait_all(col_buf.at[k], n_patch, col_send.at[k], col_recv.at[k])

    def row_pass(it):
        a_row = 1.0 / jnp.sum(col_buf[it], axis=0)

        def body(i, carry):
            ea = e_ref[block(i), :] * a_row
            if it + 1 == ITERS:
                e_ref[block(i), :] = ea
            row_buf[it, me_p, :, block(i)] = to_row(jnp.sum(ea, axis=1, keepdims=True), eye)
            return carry

        if it + 1 == ITERS and whole_blocks:
            at = block(2 * place(0) + other)
            ds_ref[at, :] = spread(e_ref[at, :] * a_row)
        lax.fori_loop(0, images, body, 0, unroll=U_P)
        send_rows(it)

    def col_pass(it):
        loss_ref[...] = 1.0 / jnp.sum(row_buf[it], axis=0)
        acc = column_pass(lambda i: loss_ref[:, block(i)], zero)
        col_buf[it + 1, me_q, :, :] = jnp.sum(acc, axis=0, keepdims=True)
        send_cols(it + 1)

    send_cols(0)
    lax.fori_loop(0, images, student_rows, 0, unroll=U_S)
    if whole_blocks:
        student_block(2 * place(0) + other, 0)
    wait_cols(0)

    row_pass(0)
    if whole_blocks:
        a_block(2 * place(0) + other, 0)
        a_pair(place(0), 2 if ahead else 1)
        student_block(2 * place(1) + other, 0)
        a_block(2 * place(1) + other, 0)
        a_pair(place(1))
        for j in range(2, half):
            student_block(2 * place(j) + other, 0)
        student_block(lo, 0)
    else:
        lax.fori_loop(0, images, student_block, 0, unroll=U_S)
    wait_rows(0)
    col_pass(0)
    if whole_blocks:
        for j in range(1, half):
            student_block(2 * j + lo, 0)
    wait_cols(1)

    row_pass(1)
    send_rows(TOTAL)
    if whole_blocks:
        for j in range(2, half):
            a_block(2 * place(j) + other, 0)
            a_pair(place(j))
        for j in range(half):
            a_block(2 * j + lo, 0)
    else:
        lax.fori_loop(0, images, a_block, 0, unroll=U_S)
        each(half, a_pair)
    wait_rows(1)
    col_pass(1)

    if ahead:
        await_bytes(feat_zero.at[place(0)], feat_zero_sem.at[2])
        for k in range(ahead):
            early(da_ref, feat_zero, 0, k)
    wait_rows(TOTAL)
    totals = jnp.sum(row_buf[TOTAL], axis=0)
    scale = 1.0 / (0.1 * rows * n_patch)
    col_buf[0, 1, :, :] = scale / totals

    def weigh(i, carry):
        t_col = to_column(col_buf[0, 1, :, block(i)], eye)
        t_ref[block(i), :] = t_col
        p_ref[block(i), :] = p_ref[block(i), :] * t_col
        return carry

    lax.fori_loop(0, images, weigh, 0, unroll=U_S)
    wait_cols(2)

    row_pass(2)

    def cross_body(i, carry):
        x = jnp.sum(e_ref[block(i), :] * s_ref[block(i), :], axis=1, keepdims=True)
        row_buf[CROSS, me_p, :, block(i)] = to_row(x, eye)
        return carry

    def cross():
        lax.fori_loop(0, images, cross_body, 0, unroll=U_S)
        send_rows(CROSS)

    if whole_blocks:
        for j in range(half):
            if j:
                b_block(2 * place(j) + other, 0)
            b_pair(place(j))
            if j == 0:
                cross()
        for j in range(half):
            b_block(2 * place(j) + lo, 0)
    else:
        lax.fori_loop(0, images, b_block, 0, unroll=U_S)
        cross()
        each(half, b_pair)

    def join(g):
        mine = part(da_ref, 2 * g + lo, piece)
        mine[...] = (mine[...] + feat_zero[g]) * part(t_ref, 2 * g + lo, piece)[...]

    if ahead:
        await_bytes(feat_zero.at[pl.ds(0, half - 1)], feat_zero_sem.at[1])
        for k in range(ahead, subs):
            mine = sub_part(da_ref, 2 * place(0) + lo, k)
            got = feat_zero[place(0), pl.ds(k * sub, sub), :]
            mine[...] = (mine[...] + got) * sub_part(t_ref, 2 * place(0) + lo, k)[...]
        for j in range(1, half):
            join(place(j))
        for k in range(ahead):
            await_bytes(sub_slot(feat_one, place(0), k), feat_one_recv.at[place(0), k])
            early(ds_ref, feat_one, 1, k)
    else:
        await_bytes(feat_zero, feat_zero_sem.at[1])
        each(half, join)
    wait_rows(2)
    b_row = 1.0 / jnp.sum(row_buf[2], axis=0)
    col_buf[0, 0, :, :] = b_row * scale

    def to_b(i, carry):
        b_ref[block(i), :] = to_column(col_buf[0, 0, :, block(i)], eye)
        return carry

    lax.fori_loop(0, images, to_b, 0, unroll=U_P)

    def feat_add(o_hi, k):
        await_bytes(sub_slot(feat_one, o_hi, k), feat_one_recv.at[o_hi, k])
        o = o_hi * 2 + lo
        both = sub_part(ds_ref, o, k)[...] + feat_one[o_hi, pl.ds(k * sub, sub), :]
        return sub_part(da_ref, o, k)[...] - sub_part(b_ref, o, k)[...] * both

    def feat_send(o_hi, k):
        remote(
            sub_part(da_ref, o_hi * 2 + lo, k),
            sub_slot(feat_two, hi, k),
            feat_two_sem.at[0],
            feat_two_sem.at[1],
            "proto",
            o_hi * 2 + lo,
        ).start()

    def direct(j, k):
        o_hi = far_first(j)
        sub_part(da_ref, o_hi * 2 + lo, k)[...] = feat_add(o_hi, k)
        feat_send(o_hi, k)

    k_piece = width // n_patch
    q_half = n_patch // 2
    q_hi, q_lo = me_q // 2, lax.rem(me_q, 2)
    q_other = 1 - q_lo

    def w_slab(ref, o, j):
        return ref.at[
            pl.ds(pl.multiple_of(o * k_piece, k_piece), k_piece), pl.ds(j * chunk, chunk)
        ]

    def dw_chunk(j):
        at = pl.ds(j * chunk, chunk)
        g = (p_ref[:, at] - e_ref[:, at] * b_ref[...]).astype(BF16)
        dw = jnp.dot(shat_t[...], g, preferred_element_type=F32)
        dw_ref[:, at] = dw

        def w_pair(d, carry):
            o_hi = lax.rem(q_hi + d, q_half)
            remote(
                w_slab(dw_ref, o_hi * 2 + q_other, j),
                w_one.at[o_hi, :, at],
                w_sem.at[0],
                w_one_recv.at[j],
                "patch",
                q_hi * 2 + q_other,
            ).start()
            return carry

        lax.fori_loop(1, q_half + 1, w_pair, 0)
        col_buf[ITERS, me_q, :, at] = jnp.sum(
            dw * proto_ref[:, at].astype(F32), axis=0, keepdims=True
        )

    def w_rest(j):
        at = pl.ds(j * chunk, chunk)
        await_bytes(w_one.at[:, :, at], w_one_recv.at[j])

        def body(d, carry):
            o_hi = lax.rem(q_hi + d, q_half)
            mine = w_slab(dw_ref, o_hi * 2 + q_lo, j)
            mine[...] = mine[...] + w_one[o_hi, :, at]
            remote(
                mine,
                w_two.at[q_hi, :, at],
                w_sem.at[2],
                w_sem.at[3],
                "patch",
                o_hi * 2 + q_lo,
            ).start()
            return carry

        lax.fori_loop(1, q_half, body, 0)

    if whole_blocks:
        for k in range(ahead, ahead + (subs - ahead) // 2):
            direct(0, k)
    for j in range(cols // chunk):
        dw_chunk(j)
    dots = col_buf.at[ITERS]
    send_cols(ITERS)
    if whole_blocks:
        for k in range(ahead + (subs - ahead) // 2, subs):
            direct(0, k)
    for j in range(cols // chunk):
        w_rest(j)
    def all_direct(j, carry):
        for k in range(subs):
            direct(j, k)
        return carry

    lax.fori_loop(1 if whole_blocks else 0, half - 1, all_direct, 0)
    x = part(rows_ref, me_p, piece)[...]
    r = lax.rsqrt(jnp.sum(x * x, axis=1, keepdims=True) + 1e-12)
    await_bytes(w_one, w_sem.at[0])
    await_bytes(feat_zero, feat_zero_sem.at[0])
    w_two[q_hi, :, :] = part(dw_ref, me_q, k_piece)[...] + w_one[q_hi]
    for k in range(subs):
        feat_two[hi, pl.ds(k * sub, sub), :] = feat_add(hi, k)

    wait_all(dots, n_patch, col_send.at[ITERS], col_recv.at[ITERS])
    await_bytes(w_two.at[pl.ds(0, q_half - 1)], w_sem.at[3])
    wait_rows(CROSS)
    loss_ref[...] = jnp.log(totals) - 10.0 * jnp.sum(row_buf[CROSS], axis=0) * b_row
    dot = jnp.sum(col_buf[ITERS], axis=0)
    r_w = rw_ref[...]
    w_mine = part(proto_ref, me_q, k_piece)[...].astype(F32)
    gp_ref[...] = r_w * jnp.sum(w_two[...], axis=0) - w_mine * (r_w * r_w * r_w * dot)

    if ahead:
        outer = jnp.logical_or(hi == 0, hi == half - 1)

        @pl.when(outer)
        def _():
            for out in range(2):
                await_bytes(early_buf.at[out], early_sem.at[out, 1])
            top = pl.ds(pl.multiple_of(me_p * piece, piece), head)
            a_part = t_ref[top, :] * jnp.sum(early_buf[0], axis=0)
            b_part = b_ref[top, :] * jnp.sum(early_buf[1], axis=0)
            source = 2 * (1 - upper)
            feat_two[source, pl.ds(0, head), :] = a_part
            feat_two[source + 1, pl.ds(0, head), :] = -b_part
            await_bytes(feat_two.at[pl.ds(0, 2)], feat_two_sem.at[1])

        @pl.when(jnp.logical_not(outer))
        def _():
            await_bytes(feat_two.at[pl.ds(0, 3)], feat_two_sem.at[1])

    else:
        await_bytes(feat_two.at[pl.ds(0, half - 1)], feat_two_sem.at[1])
    g = jnp.sum(feat_two[...], axis=0)
    gs_ref[...] = r * g - x * (r * r * r * jnp.sum(x * g, axis=1, keepdims=True))

    await_bytes(w_two.at[pl.ds(0, q_half - 1)], w_sem.at[2])
    await_bytes(feat_one, feat_one_send)
    if ahead:
        for out in range(2):
            await_bytes(early_buf.at[out, 0], early_sem.at[out, 0])
        await_bytes(feat_two.at[0, pl.ds(0, piece - head), :], feat_two_sem.at[0])
        await_bytes(feat_two.at[pl.ds(0, half - 2)], feat_two_sem.at[0])
    else:
        await_bytes(feat_two.at[pl.ds(0, half - 1)], feat_two_sem.at[0])


def finish(loss_in, gs_in, gp_in, loss_ref, gs_ref, gp_ref):
    loss_ref[...] = loss_in[...].reshape(loss_ref.shape)
    gs_ref[...] = gs_in[...]
    gp_ref[...] = gp_in[...]


def solution(mesh):
    n_proto, n_patch = mesh.shape["proto"], mesh.shape["patch"]

    def shards(teacher_feats, student_feats, masked, progress_counter, prototypes):
        images, slots = masked.shape
        rows = images * slots
        width, cols = prototypes.shape
        piece, k_piece = rows // n_proto, width // n_patch
        subs = SUBS if piece % (8 * SUBS) == 0 else 1
        vmem = pl.BlockSpec(memory_space=pltpu.VMEM)
        held = pl.pallas_call(
            functools.partial(kernel, n_proto, n_patch),
            out_shape=(
                pltpu.VMEM((1, rows), F32),
                pltpu.VMEM((piece, width), F32),
                pltpu.VMEM((k_piece, cols), F32),
            ),
            in_specs=[pl.BlockSpec(memory_space=pltpu.HBM)] * 5,
            out_specs=(vmem, vmem, vmem),
            scratch_shapes=[
                pltpu.VMEM((1, 1), jnp.int32),
                pltpu.VMEM(teacher_feats.shape, BF16),
                pltpu.VMEM(student_feats.shape, BF16),
                pltpu.VMEM(masked.shape, jnp.int32),
                pltpu.VMEM(prototypes.shape, BF16),
                pltpu.VMEM((1, cols), F32),
                pltpu.SemaphoreType.DMA((5,)),
                pltpu.VMEM((width, cols), BF16),
                pltpu.VMEM((rows, cols), F32),
                pltpu.VMEM((rows, cols), F32),
                pltpu.VMEM((rows, cols), F32),
                pltpu.VMEM((rows, cols), BF16),
                pltpu.VMEM((rows, width), F32),
                pltpu.VMEM((width, rows), BF16),
                pltpu.VMEM((rows, width), F32),
                pltpu.VMEM((width, cols), F32),
                pltpu.VMEM((rows, width), BF16),
                pltpu.VMEM((rows, width), BF16),
                pltpu.VMEM((1, cols), F32),
                pltpu.VMEM((rows, width), F32),
                pltpu.VMEM((rows, 1), F32),
                pltpu.VMEM((rows, 1), F32),
                pltpu.VMEM((n_proto // 2, piece, width), F32),
                pltpu.SemaphoreType.DMA((3,)),
                pltpu.VMEM((ITERS + 1, n_patch, 1, cols), F32),
                pltpu.VMEM((ITERS + 2, n_proto, 1, rows), F32),
                pltpu.VMEM((n_proto // 2, piece, width), F32),
                pltpu.VMEM((n_proto // 2, piece, width), F32),
                pltpu.VMEM((n_patch // 2, k_piece, cols), F32),
                pltpu.VMEM((n_patch // 2, k_piece, cols), F32),
                pltpu.SemaphoreType.DMA((ITERS + 1,)),
                pltpu.SemaphoreType.DMA((ITERS + 1,)),
                pltpu.SemaphoreType.DMA((ITERS + 2,)),
                pltpu.SemaphoreType.DMA((ITERS + 2,)),
                pltpu.SemaphoreType.DMA,
                pltpu.SemaphoreType.DMA((n_proto // 2, subs)),
                pltpu.SemaphoreType.DMA((2,)),
                pltpu.VMEM((2, 2, max(8, subs // 2 * (piece // subs)), width), F32),
                pltpu.SemaphoreType.DMA((2, 2)),
                pltpu.SemaphoreType.DMA((4,)),
                pltpu.SemaphoreType.DMA((4,)),
            ],
            compiler_params=pltpu.CompilerParams(
                collective_id=0, has_side_effects=True, vmem_limit_bytes=VLIM << 20
            ),
        )(progress_counter.reshape(1, 1), teacher_feats, student_feats, masked, prototypes)
        return tuple(
            pl.pallas_call(
                finish,
                out_shape=(
                    jax.ShapeDtypeStruct((rows,), F32),
                    jax.ShapeDtypeStruct((piece, width), F32),
                    jax.ShapeDtypeStruct((k_piece, cols), F32),
                ),
                in_specs=[vmem] * 3,
                out_specs=(vmem,) * 3,
            )(*(pltpu.with_memory_space_constraint(x, pltpu.VMEM) for x in held))
        )

    in_specs = (P("patch", None), P("patch", None), P("patch", None), P(), P(None, "proto"))
    out_specs = (P("patch"), P(("patch", "proto"), None), P("patch", "proto"))
    return jax.shard_map(shards, mesh=mesh, in_specs=in_specs, out_specs=out_specs, check_vma=False)
```
